32 devices in a mesh: lon: 8 (over z, y), lat: 4 (over x, core).
Axes of the slice: x: 2, y: 2, z: 4, core: 2. Of those that a mesh axis runs over, the one named last changes fastest.
Arguments:
- state: float32 [32, 512, 6, 128], P('lat', 'lon'), may hold values from -4 to 4
- background: float32 [32, 512, 6, 128], P('lat', 'lon'), may hold values from -4 to 4
- diffusivity: float32 [32, 512, 128], P('lat', 'lon'), may hold values from 0.03 to 0.2
- radiances: bfloat16 [2, 32, 512, 512], P(None, 'lat', 'lon'), may hold values from -5 to 5
- owners: int32 [2, 4, 32], P(None, 'lat', 'lon'), may hold values from 0 to 7, as said below
- first_layer: bfloat16 [8, 768, 1024], P('lon'), may hold values from -0.21875 to 0.21875
- second_layer: bfloat16 [8, 1024, 1024], P('lon'), may hold values from -0.1875 to 0.1875
- third_layer: bfloat16 [8, 1024, 512], P('lon'), may hold values from -0.1875 to 0.1875
- channel_weight: float32 [8, 512], P('lon'), may hold values from 0.3 to 3
Outputs:
- gradient: float32 [32, 512, 6, 128], P('lat', 'lon')
The draws below stay inside these ranges and needn't reach their ends.
Inputs may be any that keep to these rules, and one draw needn't show every extreme that they name: `owners`: every block is observed by one instrument in every slot. In each slot a device sends at most 1 of its blocks to one instrument, and an instrument receives at most 6 blocks from the devices of one latitude index; both bounds are reached in every slot and latitude index.
All inputs are finite; a program needn't handle non-finite values.
Results may differ from the reference program's by a relative error of at most 0.0024.
Values may be sent and summed in bfloat16 or wider, within the bound.
No kernel may reach another device: no remote copies, remote signals or barrier semaphores. Data moves between devices by JAX's collectives and lax.ppermute only.
A program may use at most 128 MiB of HBM per device.

```python
import math
import jax
import jax.numpy as jnp
from jax import lax

F = 6
LEV = 128
CIN = 768
H1 = 1024
H2 = 1024
CH = 512
CLAT = 8
CLON = 64
SLOTS = 2
BLK = 128
NB = 4
INSTR = 8
NLAT = 32
NLON = 512
N_LON = 8
N_LAT = 4


def draw_owners(key, part):
    stride = N_LON // NB
    extra = NB // 2
    row_keys = jax.random.split(jax.random.fold_in(key, 7), SLOTS * N_LAT)

    def one_row(row_key):
        key_relabel, key_offset, key_hot, key_score, key_order = jax.random.split(row_key, 5)
        relabel = jax.random.permutation(key_relabel, N_LON).astype(jnp.int32)
        offset = jax.random.permutation(key_offset, N_LON).astype(jnp.int32)
        hottest = jax.random.randint(key_hot, (), 0, N_LON, dtype=jnp.int32)
        block_steps = jnp.arange(NB, dtype=jnp.int32) * stride
        target = (offset[:, None] + block_steps[None, :]) % N_LON
        apart = (hottest - offset) % stride != 0
        eligible = (offset != hottest) & (apart | (stride == 1))
        score = jax.random.permutation(key_score, N_LON).astype(jnp.int32) + jnp.where(eligible, N_LON, 0)
        standing = jnp.sum(score[None, :] > score[:, None], axis=1)
        chosen = standing < extra
        target = target.at[:, 0].set(jnp.where(chosen, hottest, target[:, 0]))
        owner_ids = relabel[target]
        order_keys = jax.random.split(key_order, N_LON)
        shuffles = jax.vmap(lambda shuffle_key: jax.random.permutation(shuffle_key, NB))(order_keys)
        mixed = jnp.take_along_axis(owner_ids, shuffles.astype(jnp.int32), axis=1)
        return mixed.reshape(N_LON * NB).astype(jnp.int32)
    owner_rows = jax.vmap(one_row)(row_keys)
    return owner_rows.reshape(SLOTS, N_LAT, N_LON * NB)


def shard_levels(rng, extent, shards, low, top_value):
    gain = 1.0
    for axis_at, blocks in shards:
        draws = jax.random.uniform(jax.random.fold_in(jax.random.fold_in(rng, 6), axis_at), (blocks,), jnp.float32, low / len(shards), top_value / len(shards))
        gain = gain * jnp.repeat(jnp.exp(draws), extent[axis_at] // blocks).reshape((-1,) + (1,) * (len(extent) - 1 - axis_at))
    return gain


def centred(rng, shape, deviation, bound, cuts=(), held_as=jnp.bfloat16):
    result = deviation * jax.random.normal(rng, shape, jnp.float32)
    if cuts:
        result = result * shard_levels(rng, shape, cuts, -0.22, 0.18)
    return jnp.clip(result, -bound, bound).astype(held_as)


def setup_inputs(seed: int = 0) -> dict:
    key_list = jax.random.split(jax.random.key(seed), 10)
    state = centred(key_list[0], (NLAT, NLON, F, LEV), 1.0, 4.0, ((0, 4), (1, 8)), jnp.float32)
    background = centred(key_list[1], (NLAT, NLON, F, LEV), 1.0, 4.0, ((0, 4), (1, 8)), jnp.float32)
    diffusivity = jnp.clip(jnp.exp(math.log(0.2) - 1.89712 * jax.random.uniform(key_list[2], (NLAT, NLON, LEV), jnp.float32) ** shard_levels(key_list[2], (NLAT, NLON, LEV), ((0, 4), (1, 8)), -0.2, 0.2)), 0.03, 0.2)
    radiances = centred(key_list[3], (SLOTS, NLAT, NLON, CH), 1.0, 5.0, ((1, 4), (2, 8)))
    owners = draw_owners(jax.random.fold_in(key_list[9], 71), 0)
    first_layer = centred(key_list[5], (INSTR, CIN, H1), CIN ** -0.5, 0.21875, ((0, 8),))
    second_layer = centred(key_list[6], (INSTR, H1, H2), H1 ** -0.5, 0.1875, ((0, 8),))
    third_layer = centred(key_list[7], (INSTR, H2, CH), H2 ** -0.5, 0.1875, ((0, 8),))
    channel_weight = jnp.clip(jnp.exp(math.log(3.0) - 2.3025851 * jax.random.uniform(key_list[8], (INSTR, CH), jnp.float32) ** shard_levels(key_list[8], (INSTR, CH), ((0, 8),), -0.2, 0.2)), 0.3, 3.0)
    return {"state": state, "background": background, "diffusivity": diffusivity, "radiances": radiances, "owners": owners, "first_layer": first_layer, "second_layer": second_layer, "third_layer": third_layer, "channel_weight": channel_weight}


ADVECTION = 0.25
VERTICAL = 0.1

def stencil(padded, kappa):
    centre = padded[1:-1, 1:-1]
    northern = padded[2:, 1:-1]
    southern = padded[:-2, 1:-1]
    eastern = padded[1:-1, 2:]
    western = padded[1:-1, :-2]
    zonal_wind = centre[:, :, 0:1]
    meridional = centre[:, :, 1:2]
    transport = 0.5 * ADVECTION * (zonal_wind * (eastern - western) + meridional * (northern - southern))
    spread = eastern + western + northern + southern - 4.0 * centre
    zero_level = jnp.zeros_like(centre[..., :1])
    upper_level = jnp.concatenate([centre[..., 1:], zero_level], axis=-1)
    lower_level = jnp.concatenate([zero_level, centre[..., :-1]], axis=-1)
    return centre - transport + kappa[:, :, None, :] * spread + VERTICAL * (upper_level + lower_level - 2.0 * centre)

def advance(field, kappa):
    padded = jnp.pad(field, ((1, 1), (0, 0), (0, 0), (0, 0)))
    padded = jnp.concatenate([padded[:, -1:], padded, padded[:, :1]], axis=1)
    return stencil(padded, kappa)

def slope(values):
    sigma = jax.nn.sigmoid(values)
    return sigma * (1.0 + values * (1.0 - sigma))

def radiance_gradient(columns, targets, active, first_matrix, second_matrix, third_matrix, channel_scale):
    pre_one = jnp.dot(columns, first_matrix, preferred_element_type=jnp.float32)
    act_one = jax.nn.silu(pre_one).astype(jnp.bfloat16)
    pre_two = jnp.dot(act_one, second_matrix, preferred_element_type=jnp.float32)
    act_two = jax.nn.silu(pre_two).astype(jnp.bfloat16)
    evolved = jnp.dot(act_two, third_matrix, preferred_element_type=jnp.float32)
    misfit = (active[:, None] * channel_scale[None, :] * (evolved - targets.astype(jnp.float32))).astype(jnp.bfloat16)
    back_two = jnp.dot(misfit, third_matrix.T, preferred_element_type=jnp.float32)
    grad_two = (back_two * slope(pre_two)).astype(jnp.bfloat16)
    back_one = jnp.dot(grad_two, second_matrix.T, preferred_element_type=jnp.float32)
    grad_one = (back_one * slope(pre_one)).astype(jnp.bfloat16)
    return jnp.dot(grad_one, first_matrix.T, preferred_element_type=jnp.float32).astype(jnp.bfloat16)

def forcing(field, targets, owner_slot, first_layer, second_layer, third_layer, channel_weight):
    width_in = F * LEV
    channels = targets.shape[-1]
    column_blocks = field.astype(jnp.bfloat16).reshape(N_LAT, CLAT, N_LON, CLON, width_in).transpose(0, 2, 1, 3, 4).reshape(-1, BLK, width_in)
    target_blocks = targets.reshape(N_LAT, CLAT, N_LON, CLON, channels).transpose(0, 2, 1, 3, 4).reshape(-1, BLK, channels)
    owner_flat = owner_slot.reshape(-1).astype(jnp.int32)

    def one_block(item):
        block_columns, block_targets, owner_id = item
        return radiance_gradient(block_columns, block_targets, jnp.ones((BLK,), jnp.float32), first_layer[owner_id], second_layer[owner_id], third_layer[owner_id], channel_weight[owner_id])
    grads = lax.map(one_block, (column_blocks, target_blocks, owner_flat))
    grads = grads.reshape(N_LAT, N_LON, CLAT, CLON, width_in).transpose(0, 2, 1, 3, 4).reshape(NLAT, NLON, F, LEV)
    return grads.astype(jnp.float32)

def reference(state, background, diffusivity, radiances, owners, first_layer, second_layer, third_layer, channel_weight):
    first_state = advance(state, diffusivity)
    second_state = advance(first_state, diffusivity)
    forcing_one = forcing(first_state, radiances[0], owners[0], first_layer, second_layer, third_layer, channel_weight)
    forcing_two = forcing(second_state, radiances[1], owners[1], first_layer, second_layer, third_layer, channel_weight)
    _, pull_one = jax.vjp(lambda field: advance(field, diffusivity), first_state)
    costate = forcing_one + pull_one(forcing_two)[0]
    _, pull_zero = jax.vjp(lambda field: advance(field, diffusivity), state)
    return state - background + pull_zero(costate)[0]
```

```python
import functools
import jax
import jax.numpy as jnp
from jax import lax
from jax.experimental import pallas as pl
from jax.experimental.pallas import tpu as pltpu
from jax.sharding import PartitionSpec as P

ADVECTION = 0.25
VERTICAL = 0.1
SERVED = 4
EDGE = 16
SIDE = 8
ANY = pl.BlockSpec(memory_space=pl.ANY)
SMEM = pl.BlockSpec(memory_space=pltpu.SMEM)
VMEM = pl.BlockSpec(memory_space=pltpu.VMEM)
F32 = jnp.float32
BF16 = jnp.bfloat16


def params(mib):
    return pltpu.CompilerParams(vmem_limit_bytes=mib << 20)


def exchange(array, axis, mask):
    count = lax.axis_size(axis)
    return lax.ppermute(array, axis, [(i, i ^ mask) for i in range(count)])


def shifted(array, axis, step, periodic):
    count = lax.axis_size(axis)
    pairs = [(i, (i + step) % count) for i in range(count)]
    if not periodic:
        pairs = [(i, j) for i, j in pairs if j == i + step]
    return lax.ppermute(array, axis, pairs)


def bits_down(size):
    bit = size // 2
    while bit:
        yield bit
        bit //= 2


def pack_kernel(pos, w1, w2, w3, scale, out, tail, sems):
    lat = pos[1]
    width = out.shape[1]
    parts = width // w3.shape[1]
    n_lat = pos_lat(w1, w2, w3, out)
    r1, r2, r3 = (w.shape[0] // n_lat for w in (w1, w2, w3))
    copies = [
        pltpu.make_async_copy(w1.at[pl.ds(lat * r1, r1)], out.at[pl.ds(0, r1)], sems.at[0]),
        pltpu.make_async_copy(w2.at[pl.ds(lat * r2, r2)], out.at[pl.ds(r1, r2)], sems.at[1]),
    ]
    piece = r3 // parts
    for j in range(parts):
        copies.append(
            pltpu.make_async_copy(
                w3.at[pl.ds(lat * r3 + j * piece, piece)],
                out.at[pl.ds(r1 + r2, piece), pl.ds(j * w3.shape[1], w3.shape[1])],
                sems.at[2 + j],
            )
        )
    for copy in copies:
        copy.start()
    whole = scale[...]
    high = whole.astype(BF16).astype(F32)
    rest = whole - high
    middle = rest.astype(BF16).astype(F32)
    low = rest - middle
    tail[...] = jnp.zeros_like(tail)
    rows = lax.broadcasted_iota(jnp.int32, (tail.shape[0], scale.shape[1]), 0)
    stacked = jnp.where(rows == 0, high, jnp.where(rows == 1, middle, low))
    tail[:, 0 : scale.shape[1]] = jnp.where(rows < 3, stacked, 0.0).astype(BF16)
    last = pltpu.make_async_copy(tail, out.at[pl.ds(r1 + r2 + piece, tail.shape[0])], sems.at[2 + parts])
    last.start()
    for copy in copies:
        copy.wait()
    last.wait()


def pos_lat(w1, w2, w3, out):
    body = out.shape[0] - 16
    return (w1.shape[0] + w2.shape[0] + w3.shape[0] * w3.shape[1] // out.shape[1]) // body


def pack_weights(pos, weights, n_lat):
    w1, w2, w3, scale = weights
    width = w1.shape[1]
    parts = width // w3.shape[1]
    rows = (w1.shape[0] + w2.shape[0] + w3.shape[0] // parts) // n_lat + 16
    return pl.pallas_call(
        pack_kernel,
        out_shape=jax.ShapeDtypeStruct((rows, width), BF16),
        in_specs=[SMEM, ANY, ANY, ANY, VMEM],
        out_specs=ANY,
        scratch_shapes=[pltpu.VMEM((16, width), BF16), pltpu.SemaphoreType.DMA((3 + parts,))],
        name="pack",
    )(pos, w1, w2, w3, scale)


def spread_weights(packed, group, n_lon, n_lat):
    found = {0: packed}
    for bit in bits_down(n_lon // group):
        for near in list(found):
            found[near | bit] = exchange(found[near], "lon", bit * group)
    gathered = {}
    for served, part in found.items():
        if served == 0:
            continue
        parts = {0: part}
        for bit in bits_down(n_lat):
            for near in list(parts):
                parts[near | bit] = exchange(parts[near], "lat", bit)
        gathered[served] = parts
    return gathered


def radiance_kernel(group, pos, table, source, *refs):
    *outs, sems = refs
    slots, served, span, _ = outs[0].shape
    count = table.shape[1]
    copies = []
    for c, out in enumerate(outs, 1):
        for s in range(slots):
            for w in range(served):
                block = table[s, pos[0] ^ (w * group + c)]
                copies.append(
                    pltpu.make_async_copy(
                        source.at[s, pl.ds(pl.multiple_of(block * span, span), span)],
                        out.at[s, w],
                        sems.at[len(copies)],
                    )
                )
    for copy in copies:
        copy.start()
    for copy in copies:
        copy.wait()


def send_radiances(pos, table, radiances, group, served, span):
    slots, _, channels = radiances.shape
    shape = jax.ShapeDtypeStruct((slots, served, span, channels), BF16)
    return pl.pallas_call(
        functools.partial(radiance_kernel, group),
        out_shape=[shape] * (group - 1),
        in_specs=[SMEM, SMEM, ANY],
        out_specs=[ANY] * (group - 1),
        scratch_shapes=[pltpu.SemaphoreType.DMA(((group - 1) * slots * served,))],
        name="pick_radiances",
    )(pos, table, radiances)


def vertical_sum(values):
    lane = lax.broadcasted_iota(jnp.int32, values.shape, 1)
    size = values.shape[1]
    upper = jnp.where(lane == size - 1, 0.0, pltpu.roll(values, size - 1, 1))
    lower = jnp.where(lane == 0, 0.0, pltpu.roll(values, 1, 1))
    return upper + lower


def step_value(centre, east, west, north, south, zonal, meridional, kappa):
    transport = 0.5 * ADVECTION * (zonal * (east - west) + meridional * (north - south))
    spread = east + west + north + south - 4.0 * centre
    return centre - transport + kappa * spread + VERTICAL * (vertical_sum(centre) - 2.0 * centre)


def forward_kernel(group, pos, table, state, kappa, south, north, west, east, wide, first, columns, *sends):
    rows, fields, width, levels = state.shape
    inner = pl.ds(EDGE, width)

    def place(r, _):
        wide[r + 2, 0:fields, inner] = state[r]
        wide[r + 2, fields, inner] = kappa[r]
        return 0

    lax.fori_loop(0, rows, place, 0)
    for r in range(2):
        wide[r, :, inner] = south[r]
        wide[rows + 2 + r, :, inner] = north[r]

    def rims(r, _):
        wide[r, :, EDGE - 2 : EDGE] = west[r]
        wide[r, :, EDGE + width : EDGE + width + 2] = east[r]
        return 0

    lax.fori_loop(0, rows + 4, rims, 0)
    low = EDGE - SIDE
    span = width + 2 * SIDE

    def first_row(r, _):
        zonal = wide[r + 1, 0, pl.ds(low, span)]
        meridional = wide[r + 1, 1, pl.ds(low, span)]
        k = wide[r + 1, fields, pl.ds(low, span)]
        for f in range(fields):
            first[r, f] = step_value(
                wide[r + 1, f, pl.ds(low, span)],
                wide[r + 1, f, pl.ds(low + 1, span)],
                wide[r + 1, f, pl.ds(low - 1, span)],
                wide[r + 2, f, pl.ds(low, span)],
                wide[r, f, pl.ds(low, span)],
                zonal,
                meridional,
                k,
            )
        return 0

    lax.fori_loop(0, rows + 2, first_row, 0)

    def second_row(r, _):
        here = pl.ds(SIDE, width)
        zonal = first[r + 1, 0, here]
        meridional = first[r + 1, 1, here]
        k = wide[r + 2, fields, inner]
        lines = pl.ds(pl.multiple_of(r * width, width), width)
        for f in range(fields):
            centre = first[r + 1, f, here]
            value = step_value(
                centre,
                first[r + 1, f, pl.ds(SIDE + 1, width)],
                first[r + 1, f, pl.ds(SIDE - 1, width)],
                first[r + 2, f, here],
                first[r, f, here],
                zonal,
                meridional,
                k,
            )
            columns[0, lines, f * levels : (f + 1) * levels] = centre.astype(BF16)
            columns[1, lines, f * levels : (f + 1) * levels] = value.astype(BF16)
        return 0

    lax.fori_loop(0, rows, second_row, 0)
    slots, served, block, _ = sends[0].shape
    for c, send in enumerate(sends, 1):
        for s in range(slots):
            for w in range(served):
                b = table[s, pos[0] ^ (w * group + c)]
                send[s, w] = columns[s, pl.ds(pl.multiple_of(b * block, block), block)]


def forward(pos, table, state, kappa, rims, group, served, block):
    rows, fields, width, levels = state.shape
    slots = table.shape[0]
    outs = [
        jax.ShapeDtypeStruct((rows + 4, fields + 1, width + 2 * EDGE, levels), F32),
        jax.ShapeDtypeStruct((rows + 2, fields, width + 2 * SIDE, levels), F32),
        jax.ShapeDtypeStruct((slots, rows * width, fields * levels), BF16),
    ] + [jax.ShapeDtypeStruct((slots, served, block, fields * levels), BF16)] * (group - 1)
    return pl.pallas_call(
        functools.partial(forward_kernel, group),
        out_shape=outs,
        in_specs=[SMEM, SMEM] + [VMEM] * 6,
        out_specs=[VMEM] * len(outs),
        compiler_params=params(40),
        name="forward",
    )(pos, table, state, kappa, *rims)


def halo_of_state(state, kappa):
    width = state.shape[2]
    joined = jnp.concatenate([state, kappa[:, None]], axis=1)
    south = shifted(joined[-2:], "lat", 1, False)
    north = shifted(joined[:2], "lat", -1, False)

    def edge(cut):
        return jnp.concatenate([south[:, :, cut], joined[:, :, cut], north[:, :, cut]], axis=0)

    west = shifted(edge(slice(width - 2, width)), "lon", 1, True)
    east = shifted(edge(slice(0, 2)), "lon", -1, True)
    return south, north, west, east


def backward_kernel(first_half, *refs):
    if first_half:
        adj, south, north, west, east, base, kappa, extra, out, lo, hi, we, ea, pad = refs
        shift, row0 = SIDE, 0
    else:
        adj, south, north, west, east, base, extra, other, out, pad = refs
        shift, row0 = EDGE, 1
    rows, fields, width, levels = adj.shape
    inner = pl.ds(EDGE, width)

    def place(r, _):
        pad[r + 1, :, inner] = adj[r].astype(F32)
        pad[r + 1, :, EDGE - 1 : EDGE] = west[r][:, None]
        pad[r + 1, :, EDGE + width : EDGE + width + 1] = east[r][:, None]
        return 0

    lax.fori_loop(0, rows, place, 0)
    pad[0, :, inner] = south[...].astype(F32)
    pad[rows + 1, :, inner] = north[...].astype(F32)
    half = 0.5 * ADVECTION

    def diffusion(r, at):
        if first_half:
            return kappa[r + 1, 0, pl.ds(EDGE + at, width)]
        return base[r + 1, fields, pl.ds(EDGE + at, width)]

    def wind(r, f, at):
        return base[r + row0, f, pl.ds(shift + at, width)]

    def row(r, _):
        c_here = (1.0 - 2.0 * VERTICAL) - 4.0 * diffusion(r + 1, 0)
        c_west = diffusion(r + 1, -1) - half * wind(r + 1, 0, -1)
        c_east = diffusion(r + 1, 1) + half * wind(r + 1, 0, 1)
        c_south = diffusion(r, 0) - half * wind(r, 1, 0)
        c_north = diffusion(r + 2, 0) + half * wind(r + 2, 1, 0)
        zonal = jnp.zeros((width, levels), F32)
        meridional = jnp.zeros((width, levels), F32)
        for f in range(fields):
            here = pad[r + 1, f, inner]
            zonal += here * (wind(r + 1, f, 1) - wind(r + 1, f, -1))
            meridional += here * (wind(r + 2, f, 0) - wind(r, f, 0))
        for f in range(fields):
            here = pad[r + 1, f, inner]
            value = (
                here * c_here
                + pad[r + 1, f, pl.ds(EDGE - 1, width)] * c_west
                + pad[r + 1, f, pl.ds(EDGE + 1, width)] * c_east
                + pad[r, f, inner] * c_south
                + pad[r + 2, f, inner] * c_north
                + VERTICAL * vertical_sum(here)
            )
            if f == 0:
                value -= half * zonal
            if f == 1:
                value -= half * meridional
            if first_half:
                value += extra[r, f].astype(F32)
                we[r, f : f + 1] = value[0:1]
                ea[r, f : f + 1] = value[width - 1 : width]
            else:
                value += extra[r, f] - other[r, f]
            out[r, f] = value
        return 0

    lax.fori_loop(0, rows, row, 0)
    if first_half:
        lo[...] = out[0]
        hi[...] = out[rows - 1]


def halo_of_adjoint(edges):
    low, high, west, east = edges
    return (
        shifted(high, "lat", 1, False),
        shifted(low, "lat", -1, False),
        shifted(east, "lon", 1, True),
        shifted(west, "lon", -1, True),
    )


def backward_first(adjoint, rims, first, wide, forcing):
    rows, fields, width, levels = adjoint.shape
    line = jax.ShapeDtypeStruct((fields, width, levels), F32)
    side = jax.ShapeDtypeStruct((rows, fields, levels), F32)
    kappa_spec = pl.BlockSpec(
        (rows + 4, 1, width + 2 * EDGE, levels), lambda i: (0, fields, 0, 0)
    )

    def whole(shape):
        return pl.BlockSpec(shape, lambda i: (0,) * len(shape))

    out, *edges = pl.pallas_call(
        functools.partial(backward_kernel, True),
        grid=(1,),
        out_shape=[jax.ShapeDtypeStruct(adjoint.shape, F32), line, line, side, side],
        in_specs=[whole(a.shape) for a in (adjoint, *rims, first)]
        + [kappa_spec, whole(forcing.shape)],
        out_specs=[whole(adjoint.shape), whole(line.shape), whole(line.shape), whole(side.shape), whole(side.shape)],
        scratch_shapes=[pltpu.VMEM((rows + 2, fields, width + 2 * EDGE, levels), F32)],
        compiler_params=params(40),
        name="backward_first",
    )(adjoint, *rims, first, wide, forcing)
    return out, edges


def backward_last(adjoint, rims, wide, state, background):
    rows, fields, width, levels = adjoint.shape
    return pl.pallas_call(
        functools.partial(backward_kernel, False),
        out_shape=jax.ShapeDtypeStruct(adjoint.shape, F32),
        in_specs=[VMEM] * 8,
        out_specs=VMEM,
        scratch_shapes=[pltpu.VMEM((rows + 2, fields, width + 2 * EDGE, levels), F32)],
        compiler_params=params(40),
        name="backward_last",
    )(adjoint, *rims, wide, state, background)


def nt_dot(a, b):
    return lax.dot_general(a, b, (((1,), (1,)), ((), ())), preferred_element_type=F32)


def instrument_kernel(group, served, n_lat, pos, table, columns, radiances, *refs):
    others = group - 1
    got_columns, refs = refs[:others], refs[others:]
    got_radiances, refs = refs[:others], refs[others:]
    own_weights = served == 0
    n_weights = 4 if own_weights else n_lat
    weights, refs = refs[:n_weights], refs[n_weights:]
    outs, refs = refs[:group], refs[group:]
    x, y, w1, w2, w3, scale, a1, s1, a2, s2, mis, sem_x, sem_y, sem_w = refs
    slots, span, _ = outs[0].shape
    tile = 256
    copies_x, copies_y = [], []
    for c in range(group):
        for s in range(slots):
            j = c * slots + s
            if c == 0:
                block = table[s, pos[0] ^ (served * group)]
                lines = pl.ds(pl.multiple_of(block * span, span), span)
                from_x, from_y = columns.at[s, lines], radiances.at[s, lines]
            else:
                from_x, from_y = got_columns[c - 1].at[s, served], got_radiances[c - 1].at[s, served]
            copies_x.append(pltpu.make_async_copy(from_x, x.at[pl.ds(j * span, span)], sem_x.at[j]))
            copies_y.append(pltpu.make_async_copy(from_y, y.at[pl.ds(j * span, span)], sem_y.at[j]))
    phases = [[], [], []]
    if own_weights:
        for k, (source, target) in enumerate(zip(weights, (w1, w2, w3))):
            phases[k].append(pltpu.make_async_copy(source, target, sem_w.at[k]))
        phases[2].append(pltpu.make_async_copy(weights[3], scale, sem_w.at[3]))
    else:
        parts = w1.shape[1] // w3.shape[1]
        r1, r2, r3 = (w.shape[0] // n_lat for w in (w1, w2, w3))
        piece = r3 // parts
        count = 0
        for near in range(n_lat):
            lat = pos[1] ^ near
            source = weights[near]

            def start(phase, src, dst):
                nonlocal count
                phases[phase].append(pltpu.make_async_copy(src, dst, sem_w.at[count]))
                count += 1

            start(0, source.at[pl.ds(0, r1)], w1.at[pl.ds(pl.multiple_of(lat * r1, 16), r1)])
            start(1, source.at[pl.ds(r1, r2)], w2.at[pl.ds(pl.multiple_of(lat * r2, 16), r2)])
            for p in range(parts):
                start(
                    2,
                    source.at[pl.ds(r1 + r2, piece), pl.ds(p * w3.shape[1], w3.shape[1])],
                    w3.at[pl.ds(pl.multiple_of(lat * r3 + p * piece, 16), piece)],
                )
            if near == 0:
                start(2, source.at[pl.ds(r1 + r2 + piece, 16), pl.ds(0, w3.shape[1])], scale)
    for copy in copies_x + phases[0] + phases[1] + phases[2] + copies_y:
        copy.start()
    for copy in copies_x + phases[0]:
        copy.wait()

    def hidden(source, weight, act, slope):
        def column(n, _):
            at = pl.ds(pl.multiple_of(n * tile, tile), tile)
            z = jnp.dot(source[...], weight[:, at], preferred_element_type=F32)
            sigma = jax.nn.sigmoid(z)
            act[:, at] = (z * sigma).astype(BF16)
            slope[:, at] = sigma * (1.0 + z * (1.0 - sigma))
            return 0

        lax.fori_loop(0, weight.shape[1] // tile, column, 0)

    hidden(x, w1, a1, s1)
    for copy in phases[1]:
        copy.wait()
    hidden(a1, w2, a2, s2)
    for copy in phases[2] + copies_y:
        copy.wait()
    if not own_weights:
        triple = scale[...].astype(F32)
        factor = triple[0:1] + triple[1:2] + triple[2:3]
    else:
        factor = scale[...]
    for n in range(w3.shape[1] // tile):
        at = slice(n * tile, (n + 1) * tile)
        evolved = jnp.dot(a2[...], w3[:, at], preferred_element_type=F32)
        mis[:, at] = (factor[:, at] * (evolved - y[:, at].astype(F32))).astype(BF16)

    def back(source, weight, slope, grad):
        def column(n, _):
            at = pl.ds(pl.multiple_of(n * tile, tile), tile)
            grad[:, at] = (nt_dot(source[...], weight[at]) * slope[:, at]).astype(BF16)
            return 0

        lax.fori_loop(0, weight.shape[0] // tile, column, 0)

    back(mis, w3, s2, a2)
    back(a2, w2, s1, a1)
    for n in range(w1.shape[0] // tile):
        at = slice(n * tile, (n + 1) * tile)
        value = nt_dot(a1[...], w1[at]).astype(BF16)
        for c in range(group):
            for s in range(slots):
                j = c * slots + s
                outs[c][s, :, at] = value[j * span : (j + 1) * span]


def instrument(pos, table, columns, radiances, got_columns, got_radiances, weights, group, served, n_lat, sizes, span):
    slots, _, cin = columns.shape
    ch = radiances.shape[2]
    h1, h2 = sizes
    lines = group * slots * span
    own = served == 0
    out = jax.ShapeDtypeStruct((slots, span, cin), BF16)
    parts = h1 // ch
    return pl.pallas_call(
        functools.partial(instrument_kernel, group, served, n_lat),
        out_shape=[out] * group,
        in_specs=[SMEM, SMEM] + [ANY] * (2 + 2 * (group - 1) + len(weights)),
        out_specs=[VMEM] * group,
        scratch_shapes=[
            pltpu.VMEM((lines, cin), BF16),
            pltpu.VMEM((lines, ch), BF16),
            pltpu.VMEM((cin, h1), BF16),
            pltpu.VMEM((h1, h2), BF16),
            pltpu.VMEM((h2, ch), BF16),
            pltpu.VMEM((1, ch), F32) if own else pltpu.VMEM((16, ch), BF16),
            pltpu.VMEM((lines, h1), BF16),
            pltpu.VMEM((lines, h1), F32),
            pltpu.VMEM((lines, h2), BF16),
            pltpu.VMEM((lines, h2), F32),
            pltpu.VMEM((lines, ch), BF16),
            pltpu.SemaphoreType.DMA((group * slots,)),
            pltpu.SemaphoreType.DMA((group * slots,)),
            pltpu.SemaphoreType.DMA((4 if own else n_lat * (2 + parts) + 1,)),
        ],
        compiler_params=params(50),
        name=f"instrument_{served}",
    )(pos, table, columns, radiances, *got_columns, *got_radiances, *weights)


def collect_kernel(slot, group, edges, pos, owners, *refs):
    outs = 5 if edges else 1
    *answers, flat = refs[: len(refs) - 1 - outs] + refs[len(refs) - 1 :]
    out, *rims = refs[len(answers) : len(answers) + outs]
    rows, fields, width, levels = out.shape
    span = answers[0].shape[1]

    def block(b, _):
        apart = owners[slot, b] ^ pos[0]
        for k, answer in enumerate(answers):

            @pl.when(apart == k)
            def _():
                flat[pl.ds(pl.multiple_of(b * span, span), span)] = answer[slot]

        return 0

    lax.fori_loop(0, rows * width // span, block, 0)

    def row(r, _):
        lines = pl.ds(pl.multiple_of(r * width, width), width)
        for f in range(fields):
            value = flat[lines, f * levels : (f + 1) * levels]
            out[r, f] = value
            if edges:
                wide = value.astype(F32)
                rims[2][r, f : f + 1] = wide[0:1]
                rims[3][r, f : f + 1] = wide[width - 1 : width]
        return 0

    lax.fori_loop(0, rows, row, 0)
    if edges:
        rims[0][...] = out[0]
        rims[1][...] = out[rows - 1]


def collect(slot, pos, owners, answers, group, shape, edges):
    rows, fields, width, levels = shape
    outs = [jax.ShapeDtypeStruct(shape, BF16)]
    if edges:
        outs += [jax.ShapeDtypeStruct((fields, width, levels), BF16)] * 2
        outs += [jax.ShapeDtypeStruct((rows, fields, levels), F32)] * 2
    return pl.pallas_call(
        functools.partial(collect_kernel, slot, group, edges),
        out_shape=outs,
        in_specs=[SMEM, SMEM] + [VMEM] * len(answers),
        out_specs=[VMEM] * len(outs),
        scratch_shapes=[pltpu.VMEM((rows * width, fields * levels), BF16)],
        compiler_params=params(40),
        name=f"collect_{slot}",
    )(pos, owners, *answers)


def shards(state, background, diffusivity, radiances, owners, first_layer, second_layer, third_layer, channel_weight):
    n_lon, n_lat = lax.axis_size("lon"), lax.axis_size("lat")
    served = min(SERVED, n_lon)
    group = n_lon // served
    slots, _, blocks = owners.shape
    rows, width, fields, levels = state.shape
    span = rows * width // blocks
    cin, h1, h2 = first_layer.shape[1], first_layer.shape[2], second_layer.shape[2]
    pos = jnp.stack([lax.axis_index("lon"), lax.axis_index("lat")]).astype(jnp.int32)
    owners = owners[:, 0]
    hits = owners[:, None, :] == jnp.arange(n_lon, dtype=jnp.int32)[None, :, None]
    table = jnp.sum(jnp.where(hits, jnp.arange(blocks, dtype=jnp.int32), 0), axis=2)
    state = state.transpose(0, 2, 1, 3)
    background = background.transpose(0, 2, 1, 3)
    radiances = radiances.reshape(slots, rows * width, -1)
    own = (first_layer[0], second_layer[0], third_layer[0], channel_weight)

    rims = halo_of_state(state, diffusivity)
    gathered = spread_weights(pack_weights(pos, own, n_lat), group, n_lon, n_lat)
    sent = send_radiances(pos, table, radiances, group, served, span)
    got_radiances = [exchange(a, "lon", c) for c, a in enumerate(sent, 1)]
    wide, first, columns, *sent = forward(pos, table, state, diffusivity, rims, group, served, span)
    got_columns = [exchange(a, "lon", c) for c, a in enumerate(sent, 1)]

    answers = []
    for w in range(served):
        weights = own if w == 0 else [gathered[w][k] for k in range(n_lat)]
        mine, *theirs = instrument(
            pos, table, columns, radiances, got_columns, got_radiances, weights, group, w, n_lat, (h1, h2), span
        )
        answers.append(mine)
        answers.extend(exchange(a, "lon", c) for c, a in enumerate(theirs, 1))
    shape = state.shape
    late, *edges = collect(1, pos, owners, answers, group, shape, True)
    (early,) = collect(0, pos, owners, answers, group, shape, False)
    costate, edges = backward_first(late, halo_of_adjoint(edges), first, wide, early)
    gradient = backward_last(costate, halo_of_adjoint(edges), wide, state, background)
    return gradient.transpose(0, 2, 1, 3)


def solution(mesh):
    placed = (
        P("lat", "lon", None, None),
        P("lat", "lon", None, None),
        P("lat", "lon", None),
        P(None, "lat", "lon", None),
        P(None, "lat", "lon"),
        P("lon", None, None),
        P("lon", None, None),
        P("lon", None, None),
        P("lon", None),
    )
    return jax.shard_map(
        shards, mesh=mesh, in_specs=placed, out_specs=P("lat", "lon", None, None), check_vma=False
    )
```

```python
import functools
import jax
import jax.numpy as jnp
from jax import lax
from jax.experimental import pallas as pl
from jax.experimental.pallas import tpu as pltpu
from jax.sharding import PartitionSpec as P

ADVECTION = 0.25
VERTICAL = 0.1
SERVED = 4
EDGE = 16
SIDE = 8
TAIL = 16
ANY = pl.BlockSpec(memory_space=pl.ANY)
SMEM = pl.BlockSpec(memory_space=pltpu.SMEM)
VMEM = pl.BlockSpec(memory_space=pltpu.VMEM)
F32 = jnp.float32
BF16 = jnp.bfloat16


def params(mib):
    return pltpu.CompilerParams(vmem_limit_bytes=mib << 20)


def exchange(array, axis, mask):
    count = lax.axis_size(axis)
    return lax.ppermute(array, axis, [(i, i ^ mask) for i in range(count)])


def shifted(array, axis, step, periodic):
    count = lax.axis_size(axis)
    pairs = [(i, (i + step) % count) for i in range(count)]
    if not periodic:
        pairs = [(i, j) for i, j in pairs if j == i + step]
    return lax.ppermute(array, axis, pairs)


def bits_down(size):
    bit = size // 2
    while bit:
        yield bit
        bit //= 2


def pack_kernel(pos, w1, w2, w3, scale, out, sems):
    lat = pos[1]
    width = out.shape[1]
    parts = width // w3.shape[1]
    n_lat = pos_lat(w1, w2, w3, out)
    r1, r2, r3 = (w.shape[0] // n_lat for w in (w1, w2, w3))
    copies = [
        pltpu.make_async_copy(w1.at[pl.ds(lat * r1, r1)], out.at[pl.ds(0, r1)], sems.at[0]),
        pltpu.make_async_copy(w2.at[pl.ds(lat * r2, r2)], out.at[pl.ds(r1, r2)], sems.at[1]),
    ]
    piece = r3 // parts
    for j in range(parts):
        copies.append(
            pltpu.make_async_copy(
                w3.at[pl.ds(lat * r3 + j * piece, piece)],
                out.at[pl.ds(r1 + r2, piece), pl.ds(j * w3.shape[1], w3.shape[1])],
                sems.at[2 + j],
            )
        )
    for copy in copies:
        copy.start()
    whole = scale[...]
    high = whole.astype(BF16).astype(F32)
    rest = whole - high
    middle = rest.astype(BF16).astype(F32)
    low = rest - middle
    tail = slice(r1 + r2 + piece, out.shape[0])
    rows = lax.broadcasted_iota(jnp.int32, (TAIL, scale.shape[1]), 0)
    stacked = jnp.where(rows == 0, high, jnp.where(rows == 1, middle, low))
    out[tail] = jnp.zeros((TAIL, width), BF16)
    out[tail, 0 : scale.shape[1]] = jnp.where(rows < 3, stacked, 0.0).astype(BF16)
    for copy in copies:
        copy.wait()


def pos_lat(w1, w2, w3, out):
    body = out.shape[0] - TAIL
    return (w1.shape[0] + w2.shape[0] + w3.shape[0] * w3.shape[1] // out.shape[1]) // body


def pack_weights(pos, weights, n_lat):
    w1, w2, w3, scale = weights
    width = w1.shape[1]
    parts = width // w3.shape[1]
    rows = (w1.shape[0] + w2.shape[0] + w3.shape[0] // parts) // n_lat + TAIL
    return pl.pallas_call(
        pack_kernel,
        out_shape=jax.ShapeDtypeStruct((rows, width), BF16),
        in_specs=[SMEM, ANY, ANY, ANY, VMEM],
        out_specs=VMEM,
        scratch_shapes=[pltpu.SemaphoreType.DMA((2 + parts,))],
        name="pack",
    )(pos, w1, w2, w3, scale)


def spread_weights(packed, group, n_lon, n_lat):
    found = {0: packed}
    bits = sorted(bits_down(n_lon // group))
    for bit in bits:
        found[bit] = exchange(packed, "lon", bit * group)
    for far in range(n_lon // group):
        if far not in found:
            bottom = far & -far
            found[far] = exchange(found[far ^ bottom], "lon", bottom * group)
    gathered = {}
    for served, part in found.items():
        if served == 0:
            continue
        parts = {0: part}
        for bit in bits_down(n_lat):
            for near in list(parts):
                parts[near | bit] = exchange(parts[near], "lat", bit)
        gathered[served] = parts
    return gathered


def radiance_kernel(group, pos, table, source, *refs):
    *outs, sems = refs
    slots, served, span, _ = outs[0].shape
    count = table.shape[1]
    copies = []
    for c, out in enumerate(outs, 1):
        for s in range(slots):
            for w in range(served):
                block = table[s, pos[0] ^ (w * group + c)]
                copies.append(
                    pltpu.make_async_copy(
                        source.at[s, pl.ds(pl.multiple_of(block * span, span), span)],
                        out.at[s, w],
                        sems.at[len(copies)],
                    )
                )
    for copy in copies:
        copy.start()
    for copy in copies:
        copy.wait()


def send_radiances(pos, table, radiances, group, served, span):
    slots, _, channels = radiances.shape
    shape = jax.ShapeDtypeStruct((slots, served, span, channels), BF16)
    return pl.pallas_call(
        functools.partial(radiance_kernel, group),
        out_shape=[shape] * (group - 1),
        in_specs=[SMEM, SMEM, ANY],
        out_specs=[VMEM] * (group - 1),
        scratch_shapes=[pltpu.SemaphoreType.DMA(((group - 1) * slots * served,))],
        name="pick_radiances",
    )(pos, table, radiances)


def vertical_sum(values):
    lane = lax.broadcasted_iota(jnp.int32, values.shape, 1)
    size = values.shape[1]
    upper = jnp.where(lane == size - 1, 0.0, pltpu.roll(values, size - 1, 1))
    lower = jnp.where(lane == 0, 0.0, pltpu.roll(values, 1, 1))
    return upper + lower


def step_value(centre, east, west, north, south, zonal, meridional, kappa):
    transport = 0.5 * ADVECTION * (zonal * (east - west) + meridional * (north - south))
    spread = east + west + north + south - 4.0 * centre
    return centre - transport + kappa * spread + VERTICAL * (vertical_sum(centre) - 2.0 * centre)


def forward_kernel(group, pos, table, state, kappa, south, north, west, east, wide, first, columns, *sends):
    rows, fields, width, levels = state.shape
    inner = pl.ds(EDGE, width)

    def place(r, _):
        wide[r + 2, 0:fields, inner] = state[r]
        wide[r + 2, fields, inner] = kappa[r]
        return 0

    lax.fori_loop(0, rows, place, 0)
    for r in range(2):
        wide[r, :, inner] = south[r]
        wide[rows + 2 + r, :, inner] = north[r]

    def rims(r, _):
        wide[r, :, EDGE - 2 : EDGE] = west[r]
        wide[r, :, EDGE + width : EDGE + width + 2] = east[r]
        return 0

    lax.fori_loop(0, rows + 4, rims, 0)
    low = EDGE - SIDE
    span = width + 2 * SIDE

    def first_row(r, _):
        zonal = wide[r + 1, 0, pl.ds(low, span)]
        meridional = wide[r + 1, 1, pl.ds(low, span)]
        k = wide[r + 1, fields, pl.ds(low, span)]
        for f in range(fields):
            first[r, f] = step_value(
                wide[r + 1, f, pl.ds(low, span)],
                wide[r + 1, f, pl.ds(low + 1, span)],
                wide[r + 1, f, pl.ds(low - 1, span)],
                wide[r + 2, f, pl.ds(low, span)],
                wide[r, f, pl.ds(low, span)],
                zonal,
                meridional,
                k,
            )
        return 0

    lax.fori_loop(0, rows + 2, first_row, 0)

    def second_row(r, _):
        here = pl.ds(SIDE, width)
        zonal = first[r + 1, 0, here]
        meridional = first[r + 1, 1, here]
        k = wide[r + 2, fields, inner]
        lines = pl.ds(pl.multiple_of(r * width, width), width)
        for f in range(fields):
            centre = first[r + 1, f, here]
            value = step_value(
                centre,
                first[r + 1, f, pl.ds(SIDE + 1, width)],
                first[r + 1, f, pl.ds(SIDE - 1, width)],
                first[r + 2, f, here],
                first[r, f, here],
                zonal,
                meridional,
                k,
            )
            columns[0, lines, f * levels : (f + 1) * levels] = centre.astype(BF16)
            columns[1, lines, f * levels : (f + 1) * levels] = value.astype(BF16)
        return 0

    lax.fori_loop(0, rows, second_row, 0)
    slots, served, block, _ = sends[0].shape
    for c, send in enumerate(sends, 1):
        for s in range(slots):
            for w in range(served):
                b = table[s, pos[0] ^ (w * group + c)]
                send[s, w] = columns[s, pl.ds(pl.multiple_of(b * block, block), block)]


def forward(pos, table, state, kappa, rims, group, served, block):
    rows, fields, width, levels = state.shape
    slots = table.shape[0]
    outs = [
        jax.ShapeDtypeStruct((rows + 4, fields + 1, width + 2 * EDGE, levels), F32),
        jax.ShapeDtypeStruct((rows + 2, fields, width + 2 * SIDE, levels), F32),
        jax.ShapeDtypeStruct((slots, rows * width, fields * levels), BF16),
    ] + [jax.ShapeDtypeStruct((slots, served, block, fields * levels), BF16)] * (group - 1)
    return pl.pallas_call(
        functools.partial(forward_kernel, group),
        out_shape=outs,
        in_specs=[SMEM, SMEM] + [VMEM] * 6,
        out_specs=[VMEM] * len(outs),
        compiler_params=params(40),
        name="forward",
    )(pos, table, state, kappa, *rims)


def halo_of_state(state, kappa):
    width = state.shape[2]
    joined = jnp.concatenate([state, kappa[:, None]], axis=1)
    south = shifted(joined[-2:], "lat", 1, False)
    north = shifted(joined[:2], "lat", -1, False)

    def edge(cut):
        return jnp.concatenate([south[:, :, cut], joined[:, :, cut], north[:, :, cut]], axis=0)

    west = shifted(edge(slice(width - 2, width)), "lon", 1, True)
    east = shifted(edge(slice(0, 2)), "lon", -1, True)
    return south, north, west, east


def backward_kernel(first_half, *refs):
    if first_half:
        adj, south, north, west, east, base, kappa, extra, out, lo, hi, we, ea, pad = refs
        shift, row0 = SIDE, 0
    else:
        adj, south, north, west, east, base, extra, other, out, pad = refs
        shift, row0 = EDGE, 1
    rows, fields, width, levels = adj.shape
    inner = pl.ds(EDGE, width)

    def place(r, _):
        pad[r + 1, :, inner] = adj[r].astype(F32)
        pad[r + 1, :, EDGE - 1 : EDGE] = west[r][:, None]
        pad[r + 1, :, EDGE + width : EDGE + width + 1] = east[r][:, None]
        return 0

    lax.fori_loop(0, rows, place, 0)
    pad[0, :, inner] = south[...].astype(F32)
    pad[rows + 1, :, inner] = north[...].astype(F32)
    half = 0.5 * ADVECTION

    def diffusion(r, at):
        if first_half:
            return kappa[r + 1, 0, pl.ds(EDGE + at, width)]
        return base[r + 1, fields, pl.ds(EDGE + at, width)]

    def wind(r, f, at):
        return base[r + row0, f, pl.ds(shift + at, width)]

    def row(r, _):
        c_here = (1.0 - 2.0 * VERTICAL) - 4.0 * diffusion(r + 1, 0)
        c_west = diffusion(r + 1, -1) - half * wind(r + 1, 0, -1)
        c_east = diffusion(r + 1, 1) + half * wind(r + 1, 0, 1)
        c_south = diffusion(r, 0) - half * wind(r, 1, 0)
        c_north = diffusion(r + 2, 0) + half * wind(r + 2, 1, 0)
        zonal = jnp.zeros((width, levels), F32)
        meridional = jnp.zeros((width, levels), F32)
        for f in range(fields):
            here = pad[r + 1, f, inner]
            zonal += here * (wind(r + 1, f, 1) - wind(r + 1, f, -1))
            meridional += here * (wind(r + 2, f, 0) - wind(r, f, 0))
        for f in range(fields):
            here = pad[r + 1, f, inner]
            value = (
                here * c_here
                + pad[r + 1, f, pl.ds(EDGE - 1, width)] * c_west
                + pad[r + 1, f, pl.ds(EDGE + 1, width)] * c_east
                + pad[r, f, inner] * c_south
                + pad[r + 2, f, inner] * c_north
                + VERTICAL * vertical_sum(here)
            )
            if f == 0:
                value -= half * zonal
            if f == 1:
                value -= half * meridional
            if first_half:
                value += extra[r, f].astype(F32)
                we[r, f : f + 1] = value[0:1]
                ea[r, f : f + 1] = value[width - 1 : width]
            else:
                value += extra[r, f] - other[r, f]
            out[r, f] = value
        return 0

    lax.fori_loop(0, rows, row, 0)
    if first_half:
        lo[...] = out[0]
        hi[...] = out[rows - 1]


def halo_of_adjoint(edges):
    low, high, west, east = edges
    return (
        shifted(high, "lat", 1, False),
        shifted(low, "lat", -1, False),
        shifted(east, "lon", 1, True),
        shifted(west, "lon", -1, True),
    )


def backward_first(adjoint, rims, first, wide, forcing):
    rows, fields, width, levels = adjoint.shape
    line = jax.ShapeDtypeStruct((fields, width, levels), F32)
    side = jax.ShapeDtypeStruct((rows, fields, levels), F32)
    kappa_spec = pl.BlockSpec(
        (rows + 4, 1, width + 2 * EDGE, levels), lambda i: (0, fields, 0, 0)
    )

    def whole(shape):
        return pl.BlockSpec(shape, lambda i: (0,) * len(shape))

    out, *edges = pl.pallas_call(
        functools.partial(backward_kernel, True),
        grid=(1,),
        out_shape=[jax.ShapeDtypeStruct(adjoint.shape, F32), line, line, side, side],
        in_specs=[whole(a.shape) for a in (adjoint, *rims, first)]
        + [kappa_spec, whole(forcing.shape)],
        out_specs=[whole(adjoint.shape), whole(line.shape), whole(line.shape), whole(side.shape), whole(side.shape)],
        scratch_shapes=[pltpu.VMEM((rows + 2, fields, width + 2 * EDGE, levels), F32)],
        compiler_params=params(40),
        name="backward_first",
    )(adjoint, *rims, first, wide, forcing)
    return out, edges


def backward_last(adjoint, rims, wide, state, background):
    rows, fields, width, levels = adjoint.shape
    return pl.pallas_call(
        functools.partial(backward_kernel, False),
        out_shape=jax.ShapeDtypeStruct(adjoint.shape, F32),
        in_specs=[VMEM] * 8,
        out_specs=VMEM,
        scratch_shapes=[pltpu.VMEM((rows + 2, fields, width + 2 * EDGE, levels), F32)],
        compiler_params=params(40),
        name="backward_last",
    )(adjoint, *rims, wide, state, background)


def nt_dot(a, b):
    return lax.dot_general(a, b, (((1,), (1,)), ((), ())), preferred_element_type=F32)


def instrument_kernel(group, served, n_lat, pos, table, columns, radiances, *refs):
    others = group - 1
    got_columns, refs = refs[:others], refs[others:]
    got_radiances, refs = refs[:others], refs[others:]
    own_weights = served == 0
    n_weights = 4 if own_weights else n_lat
    weights, refs = refs[:n_weights], refs[n_weights:]
    outs, refs = refs[:group], refs[group:]
    x, y, w1, w2, w3, scale, a1, s1, a2, s2, mis, sem_x, sem_y, sem_w = refs
    slots, span, _ = outs[0].shape
    tile = 256
    copies_x, copies_y = [], []
    for c in range(group):
        for s in range(slots):
            j = c * slots + s
            if c == 0:
                block = table[s, pos[0] ^ (served * group)]
                lines = pl.ds(pl.multiple_of(block * span, span), span)
                from_x, from_y = columns.at[s, lines], radiances.at[s, lines]
            else:
                from_x, from_y = got_columns[c - 1].at[s, served], got_radiances[c - 1].at[s, served]
            copies_x.append(pltpu.make_async_copy(from_x, x.at[pl.ds(j * span, span)], sem_x.at[j]))
            copies_y.append(pltpu.make_async_copy(from_y, y.at[pl.ds(j * span, span)], sem_y.at[j]))
    phases = [[], [], []]
    if own_weights:
        for k, (source, target) in enumerate(zip(weights, (w1, w2, w3))):
            phases[k].append(pltpu.make_async_copy(source, target, sem_w.at[k]))
        phases[2].append(pltpu.make_async_copy(weights[3], scale, sem_w.at[3]))
    else:
        parts = w1.shape[1] // w3.shape[1]
        r1, r2, r3 = (w.shape[0] // n_lat for w in (w1, w2, w3))
        piece = r3 // parts
        count = 0
        for near in range(n_lat):
            lat = pos[1] ^ near
            source = weights[near]

            def start(phase, src, dst):
                nonlocal count
                phases[phase].append(pltpu.make_async_copy(src, dst, sem_w.at[count]))
                count += 1

            start(0, source.at[pl.ds(0, r1)], w1.at[pl.ds(pl.multiple_of(lat * r1, 16), r1)])
            start(1, source.at[pl.ds(r1, r2)], w2.at[pl.ds(pl.multiple_of(lat * r2, 16), r2)])
            for p in range(parts):
                start(
                    2,
                    source.at[pl.ds(r1 + r2, piece), pl.ds(p * w3.shape[1], w3.shape[1])],
                    w3.at[pl.ds(pl.multiple_of(lat * r3 + p * piece, 16), piece)],
                )
            if near == 0:
                start(2, source.at[pl.ds(r1 + r2 + piece, 16), pl.ds(0, w3.shape[1])], scale)
    for copy in copies_x + phases[0] + phases[1] + phases[2] + copies_y:
        copy.start()
    for copy in copies_x + phases[0]:
        copy.wait()

    def hidden(source, weight, act, slope):
        def column(n, _):
            at = pl.ds(pl.multiple_of(n * tile, tile), tile)
            z = jnp.dot(source[...], weight[:, at], preferred_element_type=F32)
            sigma = jax.nn.sigmoid(z)
            act[:, at] = (z * sigma).astype(BF16)
            slope[:, at] = sigma * (1.0 + z * (1.0 - sigma))
            return 0

        lax.fori_loop(0, weight.shape[1] // tile, column, 0)

    hidden(x, w1, a1, s1)
    for copy in phases[1]:
        copy.wait()
    hidden(a1, w2, a2, s2)
    for copy in phases[2] + copies_y:
        copy.wait()
    if not own_weights:
        triple = scale[...].astype(F32)
        factor = triple[0:1] + triple[1:2] + triple[2:3]
    else:
        factor = scale[...]
    for n in range(w3.shape[1] // tile):
        at = slice(n * tile, (n + 1) * tile)
        evolved = jnp.dot(a2[...], w3[:, at], preferred_element_type=F32)
        mis[:, at] = (factor[:, at] * (evolved - y[:, at].astype(F32))).astype(BF16)

    def back(source, weight, slope, grad):
        def column(n, _):
            at = pl.ds(pl.multiple_of(n * tile, tile), tile)
            grad[:, at] = (nt_dot(source[...], weight[at]) * slope[:, at]).astype(BF16)
            return 0

        lax.fori_loop(0, weight.shape[0] // tile, column, 0)

    back(mis, w3, s2, a2)
    back(a2, w2, s1, a1)
    for n in range(w1.shape[0] // tile):
        at = slice(n * tile, (n + 1) * tile)
        value = nt_dot(a1[...], w1[at]).astype(BF16)
        for c in range(group):
            for s in range(slots):
                j = c * slots + s
                outs[c][s, :, at] = value[j * span : (j + 1) * span]


def instrument(pos, table, columns, radiances, got_columns, got_radiances, weights, group, served, n_lat, sizes, span):
    slots, _, cin = columns.shape
    ch = radiances.shape[2]
    h1, h2 = sizes
    lines = group * slots * span
    own = served == 0
    out = jax.ShapeDtypeStruct((slots, span, cin), BF16)
    parts = h1 // ch
    return pl.pallas_call(
        functools.partial(instrument_kernel, group, served, n_lat),
        out_shape=[out] * group,
        in_specs=[SMEM, SMEM] + [ANY] * (2 + 2 * (group - 1) + len(weights)),
        out_specs=[VMEM] * group,
        scratch_shapes=[
            pltpu.VMEM((lines, cin), BF16),
            pltpu.VMEM((lines, ch), BF16),
            pltpu.VMEM((cin, h1), BF16),
            pltpu.VMEM((h1, h2), BF16),
            pltpu.VMEM((h2, ch), BF16),
            pltpu.VMEM((1, ch), F32) if own else pltpu.VMEM((16, ch), BF16),
            pltpu.VMEM((lines, h1), BF16),
            pltpu.VMEM((lines, h1), F32),
            pltpu.VMEM((lines, h2), BF16),
            pltpu.VMEM((lines, h2), F32),
            pltpu.VMEM((lines, ch), BF16),
            pltpu.SemaphoreType.DMA((group * slots,)),
            pltpu.SemaphoreType.DMA((group * slots,)),
            pltpu.SemaphoreType.DMA((4 if own else n_lat * (2 + parts) + 1,)),
        ],
        compiler_params=params(50),
        cost_estimate=pl.CostEstimate(
            flops=4 * lines * (cin * h1 + h1 * h2 + h2 * ch),
            transcendentals=lines * (h1 + h2),
            bytes_accessed=2 * (cin * h1 + h1 * h2 + h2 * ch + lines * (2 * cin + ch)),
        ),
        name=f"instrument_{served}",
    )(pos, table, columns, radiances, *got_columns, *got_radiances, *weights)


def collect_kernel(slot, group, edges, pos, owners, *refs):
    outs = 5 if edges else 1
    *answers, flat = refs[: len(refs) - 1 - outs] + refs[len(refs) - 1 :]
    out, *rims = refs[len(answers) : len(answers) + outs]
    rows, fields, width, levels = out.shape
    span = answers[0].shape[1]

    def block(b, _):
        apart = owners[slot, b] ^ pos[0]
        for k, answer in enumerate(answers):

            @pl.when(apart == k)
            def _():
                flat[pl.ds(pl.multiple_of(b * span, span), span)] = answer[slot]

        return 0

    lax.fori_loop(0, rows * width // span, block, 0)

    def row(r, _):
        lines = pl.ds(pl.multiple_of(r * width, width), width)
        for f in range(fields):
            value = flat[lines, f * levels : (f + 1) * levels]
            out[r, f] = value
            if edges:
                wide = value.astype(F32)
                rims[2][r, f : f + 1] = wide[0:1]
                rims[3][r, f : f + 1] = wide[width - 1 : width]
        return 0

    lax.fori_loop(0, rows, row, 0)
    if edges:
        rims[0][...] = out[0]
        rims[1][...] = out[rows - 1]


def collect(slot, pos, owners, answers, group, shape, edges):
    rows, fields, width, levels = shape
    outs = [jax.ShapeDtypeStruct(shape, BF16)]
    if edges:
        outs += [jax.ShapeDtypeStruct((fields, width, levels), BF16)] * 2
        outs += [jax.ShapeDtypeStruct((rows, fields, levels), F32)] * 2
    return pl.pallas_call(
        functools.partial(collect_kernel, slot, group, edges),
        out_shape=outs,
        in_specs=[SMEM, SMEM] + [VMEM] * len(answers),
        out_specs=[VMEM] * len(outs),
        scratch_shapes=[pltpu.VMEM((rows * width, fields * levels), BF16)],
        compiler_params=params(40),
        name=f"collect_{slot}",
    )(pos, owners, *answers)


def shards(state, background, diffusivity, radiances, owners, first_layer, second_layer, third_layer, channel_weight):
    n_lon, n_lat = lax.axis_size("lon"), lax.axis_size("lat")
    served = min(SERVED, n_lon)
    group = n_lon // served
    slots, _, blocks = owners.shape
    rows, width, fields, levels = state.shape
    span = rows * width // blocks
    cin, h1, h2 = first_layer.shape[1], first_layer.shape[2], second_layer.shape[2]
    pos = jnp.stack([lax.axis_index("lon"), lax.axis_index("lat")]).astype(jnp.int32)
    owners = owners[:, 0]
    hits = owners[:, None, :] == jnp.arange(n_lon, dtype=jnp.int32)[None, :, None]
    table = jnp.sum(jnp.where(hits, jnp.arange(blocks, dtype=jnp.int32), 0), axis=2)
    state = state.transpose(0, 2, 1, 3)
    background = background.transpose(0, 2, 1, 3)
    radiances = radiances.reshape(slots, rows * width, -1)
    own = (first_layer[0], second_layer[0], third_layer[0], channel_weight)

    rims = halo_of_state(state, diffusivity)
    gathered = spread_weights(pack_weights(pos, own, n_lat), group, n_lon, n_lat)
    sent = send_radiances(pos, table, radiances, group, served, span)
    got_radiances = [exchange(a, "lon", c) for c, a in enumerate(sent, 1)]
    wide, first, columns, *sent = forward(pos, table, state, diffusivity, rims, group, served, span)
    got_columns = [exchange(a, "lon", c) for c, a in enumerate(sent, 1)]

    answers = []
    for w in range(served):
        weights = own if w == 0 else [gathered[w][k] for k in range(n_lat)]
        mine, *theirs = instrument(
            pos, table, columns, radiances, got_columns, got_radiances, weights, group, w, n_lat, (h1, h2), span
        )
        answers.append(mine)
        answers.extend(exchange(a, "lon", c) for c, a in enumerate(theirs, 1))
    shape = state.shape
    late, *edges = collect(1, pos, owners, answers, group, shape, True)
    (early,) = collect(0, pos, owners, answers, group, shape, False)
    costate, edges = backward_first(late, halo_of_adjoint(edges), first, wide, early)
    gradient = backward_last(costate, halo_of_adjoint(edges), wide, state, background)
    return gradient.transpose(0, 2, 1, 3)


def solution(mesh):
    placed = (
        P("lat", "lon", None, None),
        P("lat", "lon", None, None),
        P("lat", "lon", None),
        P(None, "lat", "lon", None),
        P(None, "lat", "lon"),
        P("lon", None, None),
        P("lon", None, None),
        P("lon", None, None),
        P("lon", None),
    )
    return jax.shard_map(
        shards, mesh=mesh, in_specs=placed, out_specs=P("lat", "lon", None, None), check_vma=False
    )
```

```python
import functools
import jax
import jax.numpy as jnp
from jax import lax
from jax.experimental import pallas as pl
from jax.experimental.pallas import tpu as pltpu
from jax.sharding import PartitionSpec as P


ADVECTION = 0.25
VERTICAL = 0.1
SERVED = 4
EDGE = 16
SIDE = 8
CHUNKED = (1,)
TAIL = 16
ANY = pl.BlockSpec(memory_space=pl.ANY)
SMEM = pl.BlockSpec(memory_space=pltpu.SMEM)
VMEM = pl.BlockSpec(memory_space=pltpu.VMEM)
F32 = jnp.float32
BF16 = jnp.bfloat16


def params(mib):
    return pltpu.CompilerParams(vmem_limit_bytes=mib << 20)


def exchange(array, axis, mask):
    count = lax.axis_size(axis)
    return lax.ppermute(array, axis, [(i, i ^ mask) for i in range(count)])


def shifted(array, axis, step, periodic):
    count = lax.axis_size(axis)
    pairs = [(i, (i + step) % count) for i in range(count)]
    if not periodic:
        pairs = [(i, j) for i, j in pairs if j == i + step]
    return lax.ppermute(array, axis, pairs)


def bits_down(size):
    bit = size // 2
    while bit:
        yield bit
        bit //= 2


def pack_kernel(pos, w1, w2, w3, scale, out, sems):
    lat = pos[1]
    width = out.shape[1]
    parts = width // w3.shape[1]
    n_lat = pos_lat(w1, w2, w3, out)
    r1, r2, r3 = (w.shape[0] // n_lat for w in (w1, w2, w3))
    copies = [
        pltpu.make_async_copy(w1.at[pl.ds(lat * r1, r1)], out.at[pl.ds(0, r1)], sems.at[0]),
        pltpu.make_async_copy(w2.at[pl.ds(lat * r2, r2)], out.at[pl.ds(r1, r2)], sems.at[1]),
    ]
    piece = r3 // parts
    for j in range(parts):
        copies.append(
            pltpu.make_async_copy(
                w3.at[pl.ds(lat * r3 + j * piece, piece)],
                out.at[pl.ds(r1 + r2, piece), pl.ds(j * w3.shape[1], w3.shape[1])],
                sems.at[2 + j],
            )
        )
    for copy in copies:
        copy.start()
    whole = scale[...]
    high = whole.astype(BF16).astype(F32)
    rest = whole - high
    middle = rest.astype(BF16).astype(F32)
    low = rest - middle
    tail = slice(r1 + r2 + piece, out.shape[0])
    rows = lax.broadcasted_iota(jnp.int32, (TAIL, scale.shape[1]), 0)
    stacked = jnp.where(rows == 0, high, jnp.where(rows == 1, middle, low))
    out[tail] = jnp.zeros((TAIL, width), BF16)
    out[tail, 0 : scale.shape[1]] = jnp.where(rows < 3, stacked, 0.0).astype(BF16)
    for copy in copies:
        copy.wait()


def pos_lat(w1, w2, w3, out):
    body = out.shape[0] - TAIL
    return (w1.shape[0] + w2.shape[0] + w3.shape[0] * w3.shape[1] // out.shape[1]) // body


def pack_weights(pos, weights, n_lat):
    w1, w2, w3, scale = weights
    width = w1.shape[1]
    parts = width // w3.shape[1]
    rows = (w1.shape[0] + w2.shape[0] + w3.shape[0] // parts) // n_lat + TAIL
    return pl.pallas_call(
        pack_kernel,
        out_shape=jax.ShapeDtypeStruct((rows, width), BF16),
        in_specs=[SMEM, ANY, ANY, ANY, VMEM],
        out_specs=VMEM,
        scratch_shapes=[pltpu.SemaphoreType.DMA((2 + parts,))],
        name="pack",
    )(pos, w1, w2, w3, scale)


def spread_weights(packed, group, n_lon, n_lat):
    rows = packed.shape[0]
    half = rows // (2 * TAIL) * TAIL
    found = {0: (packed,)}
    bits = sorted(bits_down(n_lon // group))
    for bit in bits:
        chunks = (packed[:half], packed[half:]) if bit in CHUNKED else (packed,)
        found[bit] = tuple(exchange(a, "lon", bit * group) for a in chunks)
    for far in range(n_lon // group):
        if far not in found:
            bottom = far & -far
            found[far] = tuple(exchange(a, "lon", bottom * group) for a in found[far ^ bottom])
    gathered = {}
    for served, part in found.items():
        if served == 0:
            continue
        parts = {0: part}
        for bit in bits_down(n_lat):
            for near in list(parts):
                parts[near | bit] = tuple(exchange(a, "lat", bit) for a in parts[near])
        gathered[served] = parts
    return gathered


def radiance_kernel(group, pos, table, source, *refs):
    *outs, sems = refs
    slots, served, span, _ = outs[0].shape
    copies = []
    for c, out in enumerate(outs, 1):
        for s in range(slots):
            for w in range(served):
                block = table[s, pos[0] ^ (w * group + c)]
                copies.append(
                    pltpu.make_async_copy(
                        source.at[s, pl.ds(pl.multiple_of(block * span, span), span)],
                        out.at[s, w],
                        sems.at[len(copies)],
                    )
                )
    for copy in copies:
        copy.start()
    for copy in copies:
        copy.wait()


def send_radiances(pos, table, radiances, group, served, span):
    slots, _, channels = radiances.shape
    shape = jax.ShapeDtypeStruct((slots, served, span, channels), BF16)
    return pl.pallas_call(
        functools.partial(radiance_kernel, group),
        out_shape=[shape] * (group - 1),
        in_specs=[SMEM, SMEM, ANY],
        out_specs=[VMEM] * (group - 1),
        scratch_shapes=[pltpu.SemaphoreType.DMA(((group - 1) * slots * served,))],
        name="pick_radiances",
    )(pos, table, radiances)


def vertical_sum(values):
    lane = lax.broadcasted_iota(jnp.int32, values.shape, 1)
    size = values.shape[1]
    upper = jnp.where(lane == size - 1, 0.0, pltpu.roll(values, size - 1, 1))
    lower = jnp.where(lane == 0, 0.0, pltpu.roll(values, 1, 1))
    return upper + lower


def step_value(centre, east, west, north, south, zonal, meridional, kappa):
    transport = 0.5 * ADVECTION * (zonal * (east - west) + meridional * (north - south))
    spread = east + west + north + south - 4.0 * centre
    return centre - transport + kappa * spread + VERTICAL * (vertical_sum(centre) - 2.0 * centre)


def forward_kernel(group, pos, table, state, kappa, south, north, west, east, wide, first, columns, *sends):
    rows, fields, width, levels = state.shape
    inner = pl.ds(EDGE, width)

    def place(r, _):
        wide[r + 2, 0:fields, inner] = state[r]
        wide[r + 2, fields, inner] = kappa[r]
        return 0

    lax.fori_loop(0, rows, place, 0)
    for r in range(2):
        for target, source in ((r, south), (rows + 2 + r, north)):
            wide[target, :, inner] = source[r, :, 0:width]
            wide[target, :, EDGE - 2 : EDGE] = source[r, :, width : width + 2]
            wide[target, :, EDGE + width : EDGE + width + 2] = source[r, :, width + 2 : width + 4]

    def rims(r, _):
        wide[r + 2, :, EDGE - 2 : EDGE] = west[r]
        wide[r + 2, :, EDGE + width : EDGE + width + 2] = east[r]
        return 0

    lax.fori_loop(0, rows, rims, 0)
    low = EDGE - SIDE
    span = width + 2 * SIDE

    def first_row(r, _):
        zonal = wide[r + 1, 0, pl.ds(low, span)]
        meridional = wide[r + 1, 1, pl.ds(low, span)]
        k = wide[r + 1, fields, pl.ds(low, span)]
        for f in range(fields):
            first[r, f] = step_value(
                wide[r + 1, f, pl.ds(low, span)],
                wide[r + 1, f, pl.ds(low + 1, span)],
                wide[r + 1, f, pl.ds(low - 1, span)],
                wide[r + 2, f, pl.ds(low, span)],
                wide[r, f, pl.ds(low, span)],
                zonal,
                meridional,
                k,
            )
        return 0

    lax.fori_loop(0, rows + 2, first_row, 0)

    def second_row(r, _):
        here = pl.ds(SIDE, width)
        zonal = first[r + 1, 0, here]
        meridional = first[r + 1, 1, here]
        k = wide[r + 2, fields, inner]
        lines = pl.ds(pl.multiple_of(r * width, width), width)
        for f in range(fields):
            centre = first[r + 1, f, here]
            value = step_value(
                centre,
                first[r + 1, f, pl.ds(SIDE + 1, width)],
                first[r + 1, f, pl.ds(SIDE - 1, width)],
                first[r + 2, f, here],
                first[r, f, here],
                zonal,
                meridional,
                k,
            )
            columns[0, lines, f * levels : (f + 1) * levels] = centre.astype(BF16)
            columns[1, lines, f * levels : (f + 1) * levels] = value.astype(BF16)
        return 0

    lax.fori_loop(0, rows, second_row, 0)
    slots, served, block, _ = sends[0].shape
    for c, send in enumerate(sends, 1):
        for s in range(slots):
            for w in range(served):
                b = table[s, pos[0] ^ (w * group + c)]
                send[s, w] = columns[s, pl.ds(pl.multiple_of(b * block, block), block)]


def forward(pos, table, state, kappa, rims, group, served, block):
    rows, fields, width, levels = state.shape
    slots = table.shape[0]
    outs = [
        jax.ShapeDtypeStruct((rows + 4, fields + 1, width + 2 * EDGE, levels), F32),
        jax.ShapeDtypeStruct((rows + 2, fields, width + 2 * SIDE, levels), F32),
        jax.ShapeDtypeStruct((slots, rows * width, fields * levels), BF16),
    ] + [jax.ShapeDtypeStruct((slots, served, block, fields * levels), BF16)] * (group - 1)
    return pl.pallas_call(
        functools.partial(forward_kernel, group),
        out_shape=outs,
        in_specs=[SMEM, SMEM] + [VMEM] * 6,
        out_specs=[VMEM] * len(outs),
        compiler_params=params(40),
        name="forward",
    )(pos, table, state, kappa, *rims)


def halo_of_state(state, kappa):
    width = state.shape[2]

    def cut(rows, columns):
        return jnp.concatenate([state[rows, :, columns], kappa[rows, None, columns]], axis=1)

    every = slice(None)
    west = shifted(cut(every, slice(width - 2, width)), "lon", 1, True)
    east = shifted(cut(every, slice(0, 2)), "lon", -1, True)

    def edge(rows):
        return jnp.concatenate([cut(rows, every), west[rows], east[rows]], axis=2)

    south = shifted(edge(slice(-2, None)), "lat", 1, False)
    north = shifted(edge(slice(0, 2)), "lat", -1, False)
    return south, north, west, east


def backward_kernel(first_half, *refs):
    if first_half:
        adj, south, north, west, east, base, kappa, extra, out, lo, hi, we, ea, pad = refs
        shift, row0 = SIDE, 0
    else:
        adj, south, north, west, east, base, extra, other, out, pad = refs
        shift, row0 = EDGE, 1
    rows, fields, width, levels = adj.shape
    inner = pl.ds(EDGE, width)

    def place(r, _):
        pad[r + 1, :, inner] = adj[r].astype(F32)
        pad[r + 1, :, EDGE - 1 : EDGE] = west[r][:, None]
        pad[r + 1, :, EDGE + width : EDGE + width + 1] = east[r][:, None]
        return 0

    lax.fori_loop(0, rows, place, 0)
    pad[0, :, inner] = south[...].astype(F32)
    pad[rows + 1, :, inner] = north[...].astype(F32)
    half = 0.5 * ADVECTION

    def diffusion(r, at):
        if first_half:
            return kappa[r + 1, 0, pl.ds(EDGE + at, width)]
        return base[r + 1, fields, pl.ds(EDGE + at, width)]

    def wind(r, f, at):
        return base[r + row0, f, pl.ds(shift + at, width)]

    def row(r, _):
        c_here = (1.0 - 2.0 * VERTICAL) - 4.0 * diffusion(r + 1, 0)
        c_west = diffusion(r + 1, -1) - half * wind(r + 1, 0, -1)
        c_east = diffusion(r + 1, 1) + half * wind(r + 1, 0, 1)
        c_south = diffusion(r, 0) - half * wind(r, 1, 0)
        c_north = diffusion(r + 2, 0) + half * wind(r + 2, 1, 0)
        zonal = jnp.zeros((width, levels), F32)
        meridional = jnp.zeros((width, levels), F32)
        for f in range(fields):
            here = pad[r + 1, f, inner]
            zonal += here * (wind(r + 1, f, 1) - wind(r + 1, f, -1))
            meridional += here * (wind(r + 2, f, 0) - wind(r, f, 0))
        for f in range(fields):
            here = pad[r + 1, f, inner]
            value = (
                here * c_here
                + pad[r + 1, f, pl.ds(EDGE - 1, width)] * c_west
                + pad[r + 1, f, pl.ds(EDGE + 1, width)] * c_east
                + pad[r, f, inner] * c_south
                + pad[r + 2, f, inner] * c_north
                + VERTICAL * vertical_sum(here)
            )
            if f == 0:
                value -= half * zonal
            if f == 1:
                value -= half * meridional
            if first_half:
                value += extra[r, f].astype(F32)
                we[r, f : f + 1] = value[0:1]
                ea[r, f : f + 1] = value[width - 1 : width]
            else:
                value += extra[r, f] - other[r, f]
            out[r, f] = value
        return 0

    lax.fori_loop(0, rows, row, 0)
    if first_half:
        lo[...] = out[0]
        hi[...] = out[rows - 1]


def halo_of_adjoint(edges):
    low, high, west, east = edges
    return (
        shifted(high, "lat", 1, False),
        shifted(low, "lat", -1, False),
        shifted(east, "lon", 1, True),
        shifted(west, "lon", -1, True),
    )


def backward_first(adjoint, rims, first, wide, forcing):
    rows, fields, width, levels = adjoint.shape
    line = jax.ShapeDtypeStruct((fields, width, levels), F32)
    side = jax.ShapeDtypeStruct((rows, fields, levels), F32)
    kappa_spec = pl.BlockSpec(
        (rows + 4, 1, width + 2 * EDGE, levels), lambda i: (0, fields, 0, 0)
    )

    def whole(shape):
        return pl.BlockSpec(shape, lambda i: (0,) * len(shape))

    out, *edges = pl.pallas_call(
        functools.partial(backward_kernel, True),
        grid=(1,),
        out_shape=[jax.ShapeDtypeStruct(adjoint.shape, F32), line, line, side, side],
        in_specs=[whole(a.shape) for a in (adjoint, *rims, first)]
        + [kappa_spec, whole(forcing.shape)],
        out_specs=[whole(adjoint.shape), whole(line.shape), whole(line.shape), whole(side.shape), whole(side.shape)],
        scratch_shapes=[pltpu.VMEM((rows + 2, fields, width + 2 * EDGE, levels), F32)],
        compiler_params=params(40),
        name="backward_first",
    )(adjoint, *rims, first, wide, forcing)
    return out, edges


def backward_last(adjoint, rims, wide, state, background):
    rows, fields, width, levels = adjoint.shape
    return pl.pallas_call(
        functools.partial(backward_kernel, False),
        out_shape=jax.ShapeDtypeStruct(adjoint.shape, F32),
        in_specs=[VMEM] * 8,
        out_specs=VMEM,
        scratch_shapes=[pltpu.VMEM((rows + 2, fields, width + 2 * EDGE, levels), F32)],
        compiler_params=params(40),
        name="backward_last",
    )(adjoint, *rims, wide, state, background)


def nt_dot(a, b):
    return lax.dot_general(a, b, (((1,), (1,)), ((), ())), preferred_element_type=F32)


def instrument_kernel(group, served, n_lat, chosen, bounds, pos, table, columns, radiances, *refs):
    others = group - 1
    got_columns, refs = refs[:others], refs[others:]
    got_radiances, refs = refs[:others], refs[others:]
    own_weights = served == 0
    n_weights = 4 if own_weights else n_lat * len(bounds)
    weights, refs = refs[:n_weights], refs[n_weights:]
    outs, refs = refs[:group], refs[group:]
    x, y, w1, w2, w3, scale, a1, s1, a2, s2, mis, sem_x, sem_y, sem_w = refs
    slots, span, _ = outs[0].shape
    tile = 256
    copies_x, copies_y = [], []
    for c in range(group):
        for k, s in enumerate(chosen):
            j = c * slots + k
            if c == 0:
                block = table[s, pos[0] ^ (served * group)]
                lines = pl.ds(pl.multiple_of(block * span, span), span)
                from_x, from_y = columns.at[s, lines], radiances.at[s, lines]
            else:
                from_x, from_y = got_columns[c - 1].at[s, served], got_radiances[c - 1].at[s, served]
            copies_x.append(pltpu.make_async_copy(from_x, x.at[pl.ds(j * span, span)], sem_x.at[j]))
            copies_y.append(pltpu.make_async_copy(from_y, y.at[pl.ds(j * span, span)], sem_y.at[j]))
    phases = [[], [], []]
    if own_weights:
        for k, (source, target) in enumerate(zip(weights, (w1, w2, w3))):
            phases[k].append(pltpu.make_async_copy(source, target, sem_w.at[k]))
        phases[2].append(pltpu.make_async_copy(weights[3], scale, sem_w.at[3]))
    else:
        parts = w1.shape[1] // w3.shape[1]
        r1, r2, r3 = (w.shape[0] // n_lat for w in (w1, w2, w3))
        piece = r3 // parts
        count = 0
        for near in range(n_lat):
            lat = pos[1] ^ near
            sources = weights[near * len(bounds) : (near + 1) * len(bounds)]

            def fetch(phase, first, last, lanes, target, base):
                nonlocal count
                for source, (low, high) in zip(sources, bounds):
                    a, b = max(first, low), min(last, high)
                    if a < b:
                        begin = base + (a - first)
                        if not isinstance(begin, int):
                            begin = pl.multiple_of(begin, 16)
                        phases[phase].append(
                            pltpu.make_async_copy(
                                source.at[pl.ds(a - low, b - a), lanes],
                                target.at[pl.ds(begin, b - a)],
                                sem_w.at[count],
                            )
                        )
                        count += 1

            everything = pl.ds(0, w1.shape[1])
            ends = (r1, r1 + r2, r1 + r2 + piece)
            fetch(0, 0, ends[0], everything, w1, lat * r1)
            fetch(1, ends[0], ends[1], everything, w2, lat * r2)
            for p in range(parts):
                lanes = pl.ds(p * w3.shape[1], w3.shape[1])
                fetch(2, ends[1], ends[2], lanes, w3, lat * r3 + p * piece)
            if near == 0:
                fetch(2, ends[2], ends[2] + TAIL, pl.ds(0, w3.shape[1]), scale, 0)
    for copy in copies_x + phases[0] + phases[1] + phases[2] + copies_y:
        copy.start()
    for copy in copies_x + phases[0]:
        copy.wait()

    def hidden(source, weight, act, slope):
        def column(n, _):
            at = pl.ds(pl.multiple_of(n * tile, tile), tile)
            z = jnp.dot(source[...], weight[:, at], preferred_element_type=F32)
            half = 0.5 * jnp.tanh(0.5 * z)
            sigma = 0.5 + half
            value = z * sigma
            act[:, at] = value.astype(BF16)
            slope[:, at] = sigma + value * (0.5 - half)
            return 0

        lax.fori_loop(0, weight.shape[1] // tile, column, 0, unroll=True)

    hidden(x, w1, a1, s1)
    for copy in phases[1]:
        copy.wait()
    hidden(a1, w2, a2, s2)
    for copy in phases[2] + copies_y:
        copy.wait()
    if not own_weights:
        triple = scale[...].astype(F32)
        factor = triple[0:1] + triple[1:2] + triple[2:3]
    else:
        factor = scale[...]
    for n in range(w3.shape[1] // tile):
        at = slice(n * tile, (n + 1) * tile)
        evolved = jnp.dot(a2[...], w3[:, at], preferred_element_type=F32)
        mis[:, at] = (factor[:, at] * (evolved - y[:, at].astype(F32))).astype(BF16)

    def back(source, weight, slope, grad):
        def column(n, _):
            at = pl.ds(pl.multiple_of(n * tile, tile), tile)
            grad[:, at] = (nt_dot(source[...], weight[at]) * slope[:, at]).astype(BF16)
            return 0

        lax.fori_loop(0, weight.shape[0] // tile, column, 0, unroll=True)

    back(mis, w3, s2, a2)
    back(a2, w2, s1, a1)
    for n in range(w1.shape[0] // tile):
        at = slice(n * tile, (n + 1) * tile)
        value = nt_dot(a1[...], w1[at]).astype(BF16)
        for j in range(group * slots):
            outs[j // slots][j % slots, :, at] = value[j * span : (j + 1) * span]


def instrument(pos, table, columns, radiances, got_columns, got_radiances, weights, group, served, n_lat, sizes, span, chosen):
    cin, ch = columns.shape[2], radiances.shape[2]
    slots = len(chosen)
    h1, h2 = sizes
    own = served == 0
    bounds = []
    if not own:
        for chunk in weights[0]:
            low = bounds[-1][1] if bounds else 0
            bounds.append((low, low + chunk.shape[0]))
        weights = [chunk for near in range(n_lat) for chunk in weights[near]]
    lines = group * slots * span
    out = jax.ShapeDtypeStruct((slots, span, cin), BF16)
    parts = h1 // ch
    return pl.pallas_call(
        functools.partial(instrument_kernel, group, served, n_lat, chosen, tuple(bounds)),
        out_shape=[out] * group,
        in_specs=[SMEM, SMEM] + [ANY] * (2 + 2 * (group - 1) + len(weights)),
        out_specs=[VMEM] * group,
        scratch_shapes=[
            pltpu.VMEM((lines, cin), BF16),
            pltpu.VMEM((lines, ch), BF16),
            pltpu.VMEM((cin, h1), BF16),
            pltpu.VMEM((h1, h2), BF16),
            pltpu.VMEM((h2, ch), BF16),
            pltpu.VMEM((1, ch), F32) if own else pltpu.VMEM((16, ch), BF16),
            pltpu.VMEM((lines, h1), BF16),
            pltpu.VMEM((lines, h1), F32),
            pltpu.VMEM((lines, h2), BF16),
            pltpu.VMEM((lines, h2), F32),
            pltpu.VMEM((lines, ch), BF16),
            pltpu.SemaphoreType.DMA((group * slots,)),
            pltpu.SemaphoreType.DMA((group * slots,)),
            pltpu.SemaphoreType.DMA((4 if own else n_lat * len(bounds) * (3 + parts),)),
        ],
        compiler_params=params(50),
        cost_estimate=pl.CostEstimate(
            flops=4 * lines * (cin * h1 + h1 * h2 + h2 * ch),
            transcendentals=lines * (h1 + h2),
            bytes_accessed=2 * (cin * h1 + h1 * h2 + h2 * ch + lines * (2 * cin + ch)),
        ),
    )(pos, table, columns, radiances, *got_columns, *got_radiances, *weights)


def collect_kernel(slot, places, edges, pos, owners, *refs):
    outs = 5 if edges else 1
    *answers, flat = refs[: len(refs) - 1 - outs] + refs[len(refs) - 1 :]
    out, *rims = refs[len(answers) : len(answers) + outs]
    rows, fields, width, levels = out.shape
    span = answers[0].shape[1]

    def block(b, _):
        apart = owners[slot, b] ^ pos[0]
        for k, answer in enumerate(answers):

            @pl.when(apart == k)
            def _():
                flat[pl.ds(pl.multiple_of(b * span, span), span)] = answer[places[k]]

        return 0

    lax.fori_loop(0, rows * width // span, block, 0)

    def row(r, _):
        lines = pl.ds(pl.multiple_of(r * width, width), width)
        for f in range(fields):
            value = flat[lines, f * levels : (f + 1) * levels]
            out[r, f] = value
            if edges:
                wide = value.astype(F32)
                rims[2][r, f : f + 1] = wide[0:1]
                rims[3][r, f : f + 1] = wide[width - 1 : width]
        return 0

    lax.fori_loop(0, rows, row, 0)
    if edges:
        rims[0][...] = out[0]
        rims[1][...] = out[rows - 1]


def collect(slot, pos, owners, answers, shape, edges):
    places = tuple(place for _, place in answers)
    answers = [answer for answer, _ in answers]
    rows, fields, width, levels = shape
    outs = [jax.ShapeDtypeStruct(shape, BF16)]
    if edges:
        outs += [jax.ShapeDtypeStruct((fields, width, levels), BF16)] * 2
        outs += [jax.ShapeDtypeStruct((rows, fields, levels), F32)] * 2
    return pl.pallas_call(
        functools.partial(collect_kernel, slot, places, edges),
        out_shape=outs,
        in_specs=[SMEM, SMEM] + [VMEM] * len(answers),
        out_specs=[VMEM] * len(outs),
        scratch_shapes=[pltpu.VMEM((rows * width, fields * levels), BF16)],
        compiler_params=params(40),
    )(pos, owners, *answers)


def shards(state, background, diffusivity, radiances, owners, first_layer, second_layer, third_layer, channel_weight):
    n_lon, n_lat = lax.axis_size("lon"), lax.axis_size("lat")
    served = min(SERVED, n_lon)
    group = n_lon // served
    slots, _, blocks = owners.shape
    rows, width, _, _ = state.shape
    span = rows * width // blocks
    h1, h2 = first_layer.shape[2], second_layer.shape[2]
    pos = jnp.stack([lax.axis_index("lon"), lax.axis_index("lat")]).astype(jnp.int32)
    owners = owners[:, 0]
    hits = owners[:, None, :] == jnp.arange(n_lon, dtype=jnp.int32)[None, :, None]
    table = jnp.sum(jnp.where(hits, jnp.arange(blocks, dtype=jnp.int32), 0), axis=2)
    state = state.transpose(0, 2, 1, 3)
    background = background.transpose(0, 2, 1, 3)
    radiances = radiances.reshape(slots, rows * width, -1)
    own = (first_layer[0], second_layer[0], third_layer[0], channel_weight)

    rims = halo_of_state(state, diffusivity)
    gathered = spread_weights(pack_weights(pos, own, n_lat), group, n_lon, n_lat)
    sent = send_radiances(pos, table, radiances, group, served, span)
    got_radiances = [exchange(a, "lon", c) for c, a in enumerate(sent, 1)]
    wide, first, columns, *sent = forward(pos, table, state, diffusivity, rims, group, served, span)
    got_columns = [exchange(a, "lon", c) for c, a in enumerate(sent, 1)]

    answers = {s: [] for s in range(slots)}
    for w in range(served):
        weights = own if w == 0 else [gathered[w][k] for k in range(n_lat)]
        for chosen in [(s,) for s in reversed(range(slots))] if w == served - 1 else [tuple(range(slots))]:
            mine, *theirs = instrument(
                pos, table, columns, radiances, got_columns, got_radiances, weights, group, w, n_lat, (h1, h2), span, chosen
            )
            back = [exchange(a, "lon", c) for c, a in enumerate(theirs, 1)]
            for place, s in enumerate(chosen):
                answers[s] += [(mine, place)] + [(a, place) for a in back]
    shape = state.shape
    late, *edges = collect(1, pos, owners, answers[1], shape, True)
    (early,) = collect(0, pos, owners, answers[0], shape, False)
    costate, edges = backward_first(late, halo_of_adjoint(edges), first, wide, early)
    gradient = backward_last(costate, halo_of_adjoint(edges), wide, state, background)
    return gradient.transpose(0, 2, 1, 3)


def solution(mesh):
    placed = (
        P("lat", "lon", None, None),
        P("lat", "lon", None, None),
        P("lat", "lon", None),
        P(None, "lat", "lon", None),
        P(None, "lat", "lon"),
        P("lon", None, None),
        P("lon", None, None),
        P("lon", None, None),
        P("lon", None),
    )
    return jax.shard_map(shards, mesh=mesh, in_specs=placed, out_specs=P("lat", "lon", None, None), check_vma=False)
```

```python
import functools
import jax
import jax.numpy as jnp
from jax import lax
from jax.experimental import pallas as pl
from jax.experimental.pallas import tpu as pltpu
from jax.sharding import PartitionSpec as P


ADVECTION = 0.25
VERTICAL = 0.1
SERVED = 4
EDGE = 16
SIDE = 8
TAIL = 16
ANY = pl.BlockSpec(memory_space=pl.ANY)
SMEM = pl.BlockSpec(memory_space=pltpu.SMEM)
VMEM = pl.BlockSpec(memory_space=pltpu.VMEM)
F32 = jnp.float32
BF16 = jnp.bfloat16


def params(mib):
    return pltpu.CompilerParams(vmem_limit_bytes=mib << 20)


def exchange(array, axis, mask):
    count = lax.axis_size(axis)
    return lax.ppermute(array, axis, [(i, i ^ mask) for i in range(count)])


def shifted(array, axis, step, periodic):
    count = lax.axis_size(axis)
    pairs = [(i, (i + step) % count) for i in range(count)]
    if not periodic:
        pairs = [(i, j) for i, j in pairs if j == i + step]
    return lax.ppermute(array, axis, pairs)


def bits_down(size):
    bit = size // 2
    while bit:
        yield bit
        bit //= 2


def packed_rows(w1, w2, w3, n_lat):
    return (w1.shape[0] // n_lat, w2.shape[0] // n_lat, w3.shape[0] * w3.shape[1] // (w2.shape[1] * n_lat), TAIL)


def fetches(sources, bounds, first, last, lanes, target, base):
    for source, (low, high) in zip(sources, bounds):
        a, b = max(first, low), min(last, high)
        if a < b:
            begin = base + (a - first)
            if not isinstance(begin, int):
                begin = pl.multiple_of(begin, 16)
            yield source.at[pl.ds(a - low, b - a), lanes], target.at[pl.ds(begin, b - a)]


def pack_kernel(n_lat, bounds, pos, w1, w2, w3, scale, *refs):
    *outs, sems = refs
    lat = pos[1]
    width = outs[0].shape[1]
    r1, r2, piece, _ = packed_rows(w1, w2, w3, n_lat)
    parts = width // w3.shape[1]
    ends = (r1, r1 + r2, r1 + r2 + piece, r1 + r2 + piece + TAIL)
    copies = []

    def put(first, last, lanes, source, base):
        for at, onto in fetches(outs, bounds, first, last, lanes, source, base):
            copies.append(pltpu.make_async_copy(onto, at, sems.at[len(copies)]))

    everything = pl.ds(0, width)
    put(0, ends[0], everything, w1, lat * r1)
    put(ends[0], ends[1], everything, w2, lat * r2)
    for j in range(parts):
        put(ends[1], ends[2], pl.ds(j * w3.shape[1], w3.shape[1]), w3, (lat * parts + j) * piece)
    for copy in copies:
        copy.start()
    whole = scale[...]
    high = whole.astype(BF16).astype(F32)
    rest = whole - high
    middle = rest.astype(BF16).astype(F32)
    low = rest - middle
    rows = lax.broadcasted_iota(jnp.int32, (TAIL, scale.shape[1]), 0)
    stacked = jnp.where(rows == 0, high, jnp.where(rows == 1, middle, low))
    for out, (low_row, high_row) in zip(outs, bounds):
        if high_row == ends[3]:
            tail = slice(ends[2] - low_row, ends[3] - low_row)
            out[tail] = jnp.zeros((TAIL, width), BF16)
            out[tail, 0 : scale.shape[1]] = jnp.where(rows < 3, stacked, 0.0).astype(BF16)
    for copy in copies:
        copy.wait()


def pack_weights(pos, weights, n_lat):
    w1, w2, w3, scale = weights
    width = w1.shape[1]
    rows = sum(packed_rows(w1, w2, w3, n_lat))
    half = rows // (2 * TAIL) * TAIL
    bounds = ((0, half), (half, rows))
    return pl.pallas_call(
        functools.partial(pack_kernel, n_lat, bounds),
        out_shape=[jax.ShapeDtypeStruct((b - a, width), BF16) for a, b in bounds],
        in_specs=[SMEM, ANY, ANY, ANY, VMEM],
        out_specs=[VMEM] * len(bounds),
        scratch_shapes=[pltpu.SemaphoreType.DMA((16,))],
        name="pack",
    )(pos, w1, w2, w3, scale)


def spread_weights(packed, group, n_lon, n_lat):
    found = {0: packed}
    bits = sorted(bits_down(n_lon // group))
    for bit in bits:
        found[bit] = tuple(exchange(a, "lon", bit * group) for a in packed)
    for far in range(n_lon // group):
        if far not in found:
            bottom = far & -far
            found[far] = tuple(exchange(a, "lon", bottom * group) for a in found[far ^ bottom])
    gathered = {}
    for served, part in found.items():
        if served == 0:
            continue
        parts = {0: part}
        for bit in bits_down(n_lat):
            for near in list(parts):
                parts[near | bit] = tuple(exchange(a, "lat", bit) for a in parts[near])
        gathered[served] = parts
    return gathered


def radiance_kernel(group, pos, table, source, *outs):
    slots, served, span, _ = outs[0].shape
    for c, out in enumerate(outs, 1):
        for s in range(slots):
            for w in range(served):
                block = table[s, pos[0] ^ (w * group + c)]
                out[s, w] = source[s, pl.ds(pl.multiple_of(block * span, span), span)]


def send_radiances(pos, table, radiances, group, served, span):
    slots, _, channels = radiances.shape
    shape = jax.ShapeDtypeStruct((slots, served, span, channels), BF16)
    return pl.pallas_call(
        functools.partial(radiance_kernel, group),
        out_shape=[shape] * (group - 1),
        in_specs=[SMEM, SMEM, VMEM],
        out_specs=[VMEM] * (group - 1),
        name="pick_radiances",
    )(pos, table, radiances)


def vertical_sum(values):
    lane = lax.broadcasted_iota(jnp.int32, values.shape, 1)
    size = values.shape[1]
    upper = jnp.where(lane == size - 1, 0.0, pltpu.roll(values, size - 1, 1))
    lower = jnp.where(lane == 0, 0.0, pltpu.roll(values, 1, 1))
    return upper + lower


def step_value(centre, east, west, north, south, zonal, meridional, kappa):
    transport = 0.5 * ADVECTION * (zonal * (east - west) + meridional * (north - south))
    spread = east + west + north + south - 4.0 * centre
    return centre - transport + kappa * spread + VERTICAL * (vertical_sum(centre) - 2.0 * centre)


def forward_kernel(group, pos, table, state, kappa, south, north, west, east, wide, first, columns, *sends):
    rows, fields, width, levels = state.shape
    inner = pl.ds(EDGE, width)

    def place(r, _):
        wide[r + 2, 0:fields, inner] = state[r]
        wide[r + 2, fields, inner] = kappa[r]
        return 0

    lax.fori_loop(0, rows, place, 0)
    for r in range(2):
        for target, source in ((r, south), (rows + 2 + r, north)):
            wide[target, :, inner] = source[r, :, 0:width]
            wide[target, :, EDGE - 2 : EDGE] = source[r, :, width : width + 2]
            wide[target, :, EDGE + width : EDGE + width + 2] = source[r, :, width + 2 : width + 4]

    def rims(r, _):
        wide[r + 2, :, EDGE - 2 : EDGE] = west[r]
        wide[r + 2, :, EDGE + width : EDGE + width + 2] = east[r]
        return 0

    lax.fori_loop(0, rows, rims, 0)
    low = EDGE - SIDE
    span = width + 2 * SIDE

    def first_row(r, _):
        zonal = wide[r + 1, 0, pl.ds(low, span)]
        meridional = wide[r + 1, 1, pl.ds(low, span)]
        k = wide[r + 1, fields, pl.ds(low, span)]
        for f in range(fields):
            first[r, f] = step_value(
                wide[r + 1, f, pl.ds(low, span)],
                wide[r + 1, f, pl.ds(low + 1, span)],
                wide[r + 1, f, pl.ds(low - 1, span)],
                wide[r + 2, f, pl.ds(low, span)],
                wide[r, f, pl.ds(low, span)],
                zonal,
                meridional,
                k,
            )
        return 0

    lax.fori_loop(0, rows + 2, first_row, 0)

    def second_row(r, _):
        here = pl.ds(SIDE, width)
        zonal = first[r + 1, 0, here]
        meridional = first[r + 1, 1, here]
        k = wide[r + 2, fields, inner]
        lines = pl.ds(pl.multiple_of(r * width, width), width)
        for f in range(fields):
            centre = first[r + 1, f, here]
            value = step_value(
                centre,
                first[r + 1, f, pl.ds(SIDE + 1, width)],
                first[r + 1, f, pl.ds(SIDE - 1, width)],
                first[r + 2, f, here],
                first[r, f, here],
                zonal,
                meridional,
                k,
            )
            columns[0, lines, f * levels : (f + 1) * levels] = centre.astype(BF16)
            columns[1, lines, f * levels : (f + 1) * levels] = value.astype(BF16)
        return 0

    lax.fori_loop(0, rows, second_row, 0)
    slots, served, block, _ = sends[0].shape
    for c, send in enumerate(sends, 1):
        for s in range(slots):
            for w in range(served):
                b = table[s, pos[0] ^ (w * group + c)]
                send[s, w] = columns[s, pl.ds(pl.multiple_of(b * block, block), block)]


def forward(pos, table, state, kappa, rims, group, served, block):
    rows, fields, width, levels = state.shape
    slots = table.shape[0]
    outs = [
        jax.ShapeDtypeStruct((rows + 4, fields + 1, width + 2 * EDGE, levels), F32),
        jax.ShapeDtypeStruct((rows + 2, fields, width + 2 * SIDE, levels), F32),
        jax.ShapeDtypeStruct((slots, rows * width, fields * levels), BF16),
    ] + [jax.ShapeDtypeStruct((slots, served, block, fields * levels), BF16)] * (group - 1)
    return pl.pallas_call(
        functools.partial(forward_kernel, group),
        out_shape=outs,
        in_specs=[SMEM, SMEM] + [VMEM] * 6,
        out_specs=[VMEM] * len(outs),
        compiler_params=params(16),
        name="forward",
    )(pos, table, state, kappa, *rims)


def halo_of_state(state, kappa):
    width = state.shape[2]

    def cut(rows, columns):
        return jnp.concatenate([state[rows, :, columns], kappa[rows, None, columns]], axis=1)

    every = slice(None)
    west = shifted(cut(every, slice(width - 2, width)), "lon", 1, True)
    east = shifted(cut(every, slice(0, 2)), "lon", -1, True)

    def edge(rows):
        return jnp.concatenate([cut(rows, every), west[rows], east[rows]], axis=2)

    south = shifted(edge(slice(-2, None)), "lat", 1, False)
    north = shifted(edge(slice(0, 2)), "lat", -1, False)
    return south, north, west, east


def backward_kernel(first_half, *refs):
    if first_half:
        adj, south, north, west, east, base, kappa, extra, out, lo, hi, we, ea, pad = refs
        shift, row0 = SIDE, 0
    else:
        adj, south, north, west, east, base, extra, other, out, pad = refs
        shift, row0 = EDGE, 1
    rows, fields, width, levels = adj.shape
    inner = pl.ds(EDGE, width)

    def place(r, _):
        pad[r + 1, :, inner] = adj[r].astype(F32)
        pad[r + 1, :, EDGE - 1 : EDGE] = west[r][:, None]
        pad[r + 1, :, EDGE + width : EDGE + width + 1] = east[r][:, None]
        return 0

    lax.fori_loop(0, rows, place, 0)
    pad[0, :, inner] = south[...].astype(F32)
    pad[rows + 1, :, inner] = north[...].astype(F32)
    half = 0.5 * ADVECTION

    def diffusion(r, at):
        if first_half:
            return kappa[r + 1, 0, pl.ds(EDGE + at, width)]
        return base[r + 1, fields, pl.ds(EDGE + at, width)]

    def wind(r, f, at):
        return base[r + row0, f, pl.ds(shift + at, width)]

    def row(r, _):
        c_here = (1.0 - 2.0 * VERTICAL) - 4.0 * diffusion(r + 1, 0)
        c_west = diffusion(r + 1, -1) - half * wind(r + 1, 0, -1)
        c_east = diffusion(r + 1, 1) + half * wind(r + 1, 0, 1)
        c_south = diffusion(r, 0) - half * wind(r, 1, 0)
        c_north = diffusion(r + 2, 0) + half * wind(r + 2, 1, 0)
        zonal = jnp.zeros((width, levels), F32)
        meridional = jnp.zeros((width, levels), F32)
        for f in range(fields):
            here = pad[r + 1, f, inner]
            zonal += here * (wind(r + 1, f, 1) - wind(r + 1, f, -1))
            meridional += here * (wind(r + 2, f, 0) - wind(r, f, 0))
        for f in range(fields):
            here = pad[r + 1, f, inner]
            value = (
                here * c_here
                + pad[r + 1, f, pl.ds(EDGE - 1, width)] * c_west
                + pad[r + 1, f, pl.ds(EDGE + 1, width)] * c_east
                + pad[r, f, inner] * c_south
                + pad[r + 2, f, inner] * c_north
                + VERTICAL * vertical_sum(here)
            )
            if f == 0:
                value -= half * zonal
            if f == 1:
                value -= half * meridional
            if first_half:
                value += extra[r, f].astype(F32)
                we[r, f : f + 1] = value[0:1]
                ea[r, f : f + 1] = value[width - 1 : width]
            else:
                value += extra[r, f] - other[r, f]
            out[r, f] = value
        return 0

    lax.fori_loop(0, rows, row, 0)
    if first_half:
        lo[...] = out[0]
        hi[...] = out[rows - 1]


def halo_of_adjoint(edges):
    low, high, west, east = edges
    return (
        shifted(high, "lat", 1, False),
        shifted(low, "lat", -1, False),
        shifted(east, "lon", 1, True),
        shifted(west, "lon", -1, True),
    )


def backward_first(adjoint, rims, first, wide, forcing):
    rows, fields, width, levels = adjoint.shape
    line = jax.ShapeDtypeStruct((fields, width, levels), F32)
    side = jax.ShapeDtypeStruct((rows, fields, levels), F32)
    kappa_spec = pl.BlockSpec(
        (rows + 4, 1, width + 2 * EDGE, levels), lambda i: (0, fields, 0, 0)
    )

    def whole(shape):
        return pl.BlockSpec(shape, lambda i: (0,) * len(shape))

    out, *edges = pl.pallas_call(
        functools.partial(backward_kernel, True),
        grid=(1,),
        out_shape=[jax.ShapeDtypeStruct(adjoint.shape, F32), line, line, side, side],
        in_specs=[whole(a.shape) for a in (adjoint, *rims, first)]
        + [kappa_spec, whole(forcing.shape)],
        out_specs=[whole(adjoint.shape), whole(line.shape), whole(line.shape), whole(side.shape), whole(side.shape)],
        scratch_shapes=[pltpu.VMEM((rows + 2, fields, width + 2 * EDGE, levels), F32)],
        compiler_params=params(16),
        name="backward_first",
    )(adjoint, *rims, first, wide, forcing)
    return out, edges


def backward_last(adjoint, rims, wide, state, background):
    rows, fields, width, levels = adjoint.shape
    return pl.pallas_call(
        functools.partial(backward_kernel, False),
        out_shape=jax.ShapeDtypeStruct(adjoint.shape, F32),
        in_specs=[VMEM] * 8,
        out_specs=VMEM,
        scratch_shapes=[pltpu.VMEM((rows + 2, fields, width + 2 * EDGE, levels), F32)],
        compiler_params=params(16),
        name="backward_last",
    )(adjoint, *rims, wide, state, background)


def nt_dot(a, b):
    return lax.dot_general(a, b, (((1,), (1,)), ((), ())), preferred_element_type=F32)


def instrument_kernel(group, served, n_lat, chosen, bounds, pos, table, columns, radiances, *refs):
    others = group - 1
    got_columns, refs = refs[:others], refs[others:]
    got_radiances, refs = refs[:others], refs[others:]
    own_weights = served == 0
    n_weights = 4 if own_weights else n_lat * len(bounds)
    weights, refs = refs[:n_weights], refs[n_weights:]
    outs, refs = refs[:group], refs[group:]
    x, y, a1, s1, a2, s2, mis, *built = refs
    slots, span, _ = outs[0].shape
    tile = 256
    for c in range(group):
        for k, s in enumerate(chosen):
            j = c * slots + k
            lines = slice(j * span, (j + 1) * span)
            if c == 0:
                block = table[s, pos[0] ^ (served * group)]
                at = pl.ds(pl.multiple_of(block * span, span), span)
                x[lines] = columns[s, at]
                y[lines] = radiances[s, at]
            else:
                x[lines] = got_columns[c - 1][s, served]
                y[lines] = got_radiances[c - 1][s, served]
    if own_weights:
        w1, w2, w3, scale = weights
        factor = scale[...]
    else:
        w1, w2, w3 = built
        r1, r2, piece, _ = packed_rows(w1, w2, w3, n_lat)
        parts = w2.shape[1] // w3.shape[1]
        ends = (r1, r1 + r2, r1 + r2 + piece)
        everything = pl.ds(0, w1.shape[1])

        def fetch(first, last, lanes, target, base):
            for source, onto in fetches(sources, bounds, first, last, lanes, target, base):
                onto[...] = source[...]

        for near in range(n_lat):
            lat = pos[1] ^ near
            sources = weights[near * len(bounds) : (near + 1) * len(bounds)]
            fetch(0, ends[0], everything, w1, lat * r1)
            fetch(ends[0], ends[1], everything, w2, lat * r2)
            for p in range(parts):
                fetch(ends[1], ends[2], pl.ds(p * w3.shape[1], w3.shape[1]), w3, (lat * parts + p) * piece)
        last, low = weights[len(bounds) - 1], bounds[-1][0]
        triple = last[ends[2] - low : ends[2] - low + TAIL, 0 : w3.shape[1]].astype(F32)
        factor = triple[0:1] + triple[1:2] + triple[2:3]

    def hidden(source, weight, act, slope):
        def column(n, _):
            at = pl.ds(pl.multiple_of(n * tile, tile), tile)
            z = jnp.dot(source[...], weight[:, at], preferred_element_type=F32)
            half = 0.5 * jnp.tanh(0.5 * z)
            sigma = 0.5 + half
            value = z * sigma
            act[:, at] = value.astype(BF16)
            slope[:, at] = sigma + value * (0.5 - half)
            return 0

        lax.fori_loop(0, weight.shape[1] // tile, column, 0, unroll=True)

    hidden(x, w1, a1, s1)
    hidden(a1, w2, a2, s2)
    for n in range(w3.shape[1] // tile):
        at = slice(n * tile, (n + 1) * tile)
        evolved = jnp.dot(a2[...], w3[:, at], preferred_element_type=F32)
        mis[:, at] = (factor[:, at] * (evolved - y[:, at].astype(F32))).astype(BF16)

    def back(source, weight, slope, grad):
        def column(n, _):
            at = pl.ds(pl.multiple_of(n * tile, tile), tile)
            grad[:, at] = (nt_dot(source[...], weight[at]) * slope[:, at]).astype(BF16)
            return 0

        lax.fori_loop(0, weight.shape[0] // tile, column, 0, unroll=True)

    back(mis, w3, s2, a2)
    back(a2, w2, s1, a1)
    for n in range(w1.shape[0] // tile):
        at = slice(n * tile, (n + 1) * tile)
        value = nt_dot(a1[...], w1[at]).astype(BF16)
        for j in range(group * slots):
            outs[j // slots][j % slots, :, at] = value[j * span : (j + 1) * span]


def instrument(pos, table, columns, radiances, got_columns, got_radiances, weights, group, served, n_lat, sizes, span, chosen):
    cin, ch = columns.shape[2], radiances.shape[2]
    slots = len(chosen)
    h1, h2 = sizes
    own = served == 0
    bounds = []
    if not own:
        for chunk in weights[0]:
            low = bounds[-1][1] if bounds else 0
            bounds.append((low, low + chunk.shape[0]))
        weights = [chunk for near in range(n_lat) for chunk in weights[near]]
    lines = group * slots * span
    out = jax.ShapeDtypeStruct((slots, span, cin), BF16)
    return pl.pallas_call(
        functools.partial(instrument_kernel, group, served, n_lat, chosen, tuple(bounds)),
        out_shape=[out] * group,
        in_specs=[SMEM, SMEM] + [VMEM] * (2 + 2 * (group - 1) + len(weights)),
        out_specs=[VMEM] * group,
        scratch_shapes=[
            pltpu.VMEM((lines, cin), BF16),
            pltpu.VMEM((lines, ch), BF16),
            pltpu.VMEM((lines, h1), BF16),
            pltpu.VMEM((lines, h1), F32),
            pltpu.VMEM((lines, h2), BF16),
            pltpu.VMEM((lines, h2), F32),
            pltpu.VMEM((lines, ch), BF16),
        ]
        + ([] if own else [pltpu.VMEM(shape, BF16) for shape in ((cin, h1), (h1, h2), (h2, ch))]),
        compiler_params=params(32),
        cost_estimate=pl.CostEstimate(
            flops=4 * lines * (cin * h1 + h1 * h2 + h2 * ch),
            transcendentals=lines * (h1 + h2),
            bytes_accessed=2 * (cin * h1 + h1 * h2 + h2 * ch + lines * (2 * cin + ch)),
        ),
    )(pos, table, columns, radiances, *got_columns, *got_radiances, *weights)


def collect_kernel(slot, places, edges, pos, owners, *refs):
    outs = 5 if edges else 1
    *answers, flat = refs[: len(refs) - 1 - outs] + refs[len(refs) - 1 :]
    out, *rims = refs[len(answers) : len(answers) + outs]
    rows, fields, width, levels = out.shape
    span = answers[0].shape[1]

    def block(b, _):
        apart = owners[slot, b] ^ pos[0]
        for k, answer in enumerate(answers):

            @pl.when(apart == k)
            def _():
                flat[pl.ds(pl.multiple_of(b * span, span), span)] = answer[places[k]]

        return 0

    lax.fori_loop(0, rows * width // span, block, 0)

    def row(r, _):
        lines = pl.ds(pl.multiple_of(r * width, width), width)
        for f in range(fields):
            value = flat[lines, f * levels : (f + 1) * levels]
            out[r, f] = value
            if edges:
                wide = value.astype(F32)
                rims[2][r, f : f + 1] = wide[0:1]
                rims[3][r, f : f + 1] = wide[width - 1 : width]
        return 0

    lax.fori_loop(0, rows, row, 0)
    if edges:
        rims[0][...] = out[0]
        rims[1][...] = out[rows - 1]


def collect(slot, pos, owners, answers, shape, edges):
    places = tuple(place for _, place in answers)
    answers = [answer for answer, _ in answers]
    rows, fields, width, levels = shape
    outs = [jax.ShapeDtypeStruct(shape, BF16)]
    if edges:
        outs += [jax.ShapeDtypeStruct((fields, width, levels), BF16)] * 2
        outs += [jax.ShapeDtypeStruct((rows, fields, levels), F32)] * 2
    return pl.pallas_call(
        functools.partial(collect_kernel, slot, places, edges),
        out_shape=outs,
        in_specs=[SMEM, SMEM] + [VMEM] * len(answers),
        out_specs=[VMEM] * len(outs),
        scratch_shapes=[pltpu.VMEM((rows * width, fields * levels), BF16)],
        compiler_params=params(16),
    )(pos, owners, *answers)


def shards(state, background, diffusivity, radiances, owners, first_layer, second_layer, third_layer, channel_weight):
    n_lon, n_lat = lax.axis_size("lon"), lax.axis_size("lat")
    served = min(SERVED, n_lon)
    group = n_lon // served
    slots, _, blocks = owners.shape
    rows, width, _, _ = state.shape
    span = rows * width // blocks
    h1, h2 = first_layer.shape[2], second_layer.shape[2]
    pos = jnp.stack([lax.axis_index("lon"), lax.axis_index("lat")]).astype(jnp.int32)
    owners = owners[:, 0]
    hits = owners[:, None, :] == jnp.arange(n_lon, dtype=jnp.int32)[None, :, None]
    table = jnp.sum(jnp.where(hits, jnp.arange(blocks, dtype=jnp.int32), 0), axis=2)
    state = state.transpose(0, 2, 1, 3)
    background = background.transpose(0, 2, 1, 3)
    radiances = radiances.reshape(slots, rows * width, -1)
    own = (first_layer[0], second_layer[0], third_layer[0], channel_weight)

    rims = halo_of_state(state, diffusivity)
    gathered = spread_weights(pack_weights(pos, own, n_lat), group, n_lon, n_lat)
    sent = send_radiances(pos, table, radiances, group, served, span)
    got_radiances = [exchange(a, "lon", c) for c, a in enumerate(sent, 1)]
    wide, first, columns, *sent = forward(pos, table, state, diffusivity, rims, group, served, span)
    got_columns = [exchange(a, "lon", c) for c, a in enumerate(sent, 1)]

    answers = {s: [] for s in range(slots)}
    for w in range(served):
        weights = own if w == 0 else [gathered[w][k] for k in range(n_lat)]
        for chosen in [(s,) for s in reversed(range(slots))] if w == served - 1 else [tuple(range(slots))]:
            mine, *theirs = instrument(
                pos, table, columns, radiances, got_columns, got_radiances, weights, group, w, n_lat, (h1, h2), span, chosen
            )
            back = [exchange(a, "lon", c) for c, a in enumerate(theirs, 1)]
            for place, s in enumerate(chosen):
                answers[s] += [(mine, place)] + [(a, place) for a in back]
    shape = state.shape
    late, *edges = collect(1, pos, owners, answers[1], shape, True)
    (early,) = collect(0, pos, owners, answers[0], shape, False)
    costate, edges = backward_first(late, halo_of_adjoint(edges), first, wide, early)
    gradient = backward_last(costate, halo_of_adjoint(edges), wide, state, background)
    return gradient.transpose(0, 2, 1, 3)


def solution(mesh):
    placed = (
        P("lat", "lon", None, None),
        P("lat", "lon", None, None),
        P("lat", "lon", None),
        P(None, "lat", "lon", None),
        P(None, "lat", "lon"),
        P("lon", None, None),
        P("lon", None, None),
        P("lon", None, None),
        P("lon", None),
    )
    return jax.shard_map(shards, mesh=mesh, in_specs=placed, out_specs=P("lat", "lon", None, None), check_vma=False)
```

```python
import functools
import jax
import jax.numpy as jnp
from jax import lax
from jax.experimental import pallas as pl
from jax.experimental.pallas import tpu as pltpu
from jax.sharding import PartitionSpec as P


ADVECTION = 0.25
VERTICAL = 0.1
SERVED = 4
EDGE = 16
SIDE = 8
TAIL = 16
ANY = pl.BlockSpec(memory_space=pl.ANY)
SMEM = pl.BlockSpec(memory_space=pltpu.SMEM)
VMEM = pl.BlockSpec(memory_space=pltpu.VMEM)
F32 = jnp.float32
BF16 = jnp.bfloat16


def params(mib):
    return pltpu.CompilerParams(vmem_limit_bytes=mib << 20)


def exchange(array, axis, mask):
    count = lax.axis_size(axis)
    return lax.ppermute(array, axis, [(i, i ^ mask) for i in range(count)])


def shifted(array, axis, step, periodic):
    count = lax.axis_size(axis)
    pairs = [(i, (i + step) % count) for i in range(count)]
    if not periodic:
        pairs = [(i, j) for i, j in pairs if j == i + step]
    return lax.ppermute(array, axis, pairs)


def bits_down(size):
    bit = size // 2
    while bit:
        yield bit
        bit //= 2


def packed_rows(w1, w2, w3, n_lat):
    return (w1.shape[0] // n_lat, w2.shape[0] // n_lat, w3.shape[0] * w3.shape[1] // (w2.shape[1] * n_lat), TAIL)


def fetches(sources, bounds, first, last, lanes, target, base):
    for source, (low, high) in zip(sources, bounds):
        a, b = max(first, low), min(last, high)
        if a < b:
            begin = base + (a - first)
            if not isinstance(begin, int):
                begin = pl.multiple_of(begin, 16)
            yield source.at[pl.ds(a - low, b - a), lanes], target.at[pl.ds(begin, b - a)]


def pack_kernel(n_lat, bounds, pos, w1, w2, w3, scale, *refs):
    *outs, sems = refs
    lat = pos[1]
    width = outs[0].shape[1]
    r1, r2, piece, _ = packed_rows(w1, w2, w3, n_lat)
    parts = width // w3.shape[1]
    ends = (r1, r1 + r2, r1 + r2 + piece, r1 + r2 + piece + TAIL)
    copies = []

    def put(first, last, lanes, source, base):
        for at, onto in fetches(outs, bounds, first, last, lanes, source, base):
            copies.append(pltpu.make_async_copy(onto, at, sems.at[len(copies)]))

    everything = pl.ds(0, width)
    put(0, ends[0], everything, w1, lat * r1)
    put(ends[0], ends[1], everything, w2, lat * r2)
    for j in range(parts):
        put(ends[1], ends[2], pl.ds(j * w3.shape[1], w3.shape[1]), w3, (lat * parts + j) * piece)
    for copy in copies:
        copy.start()
    whole = scale[...]
    high = whole.astype(BF16).astype(F32)
    rest = whole - high
    middle = rest.astype(BF16).astype(F32)
    low = rest - middle
    rows = lax.broadcasted_iota(jnp.int32, (TAIL, scale.shape[1]), 0)
    stacked = jnp.where(rows == 0, high, jnp.where(rows == 1, middle, low))
    for out, (low_row, high_row) in zip(outs, bounds):
        if high_row == ends[3]:
            tail = slice(ends[2] - low_row, ends[3] - low_row)
            out[tail] = jnp.zeros((TAIL, width), BF16)
            out[tail, 0 : scale.shape[1]] = jnp.where(rows < 3, stacked, 0.0).astype(BF16)
    for copy in copies:
        copy.wait()


def pack_weights(pos, weights, n_lat):
    w1, w2, w3, scale = weights
    width = w1.shape[1]
    rows = sum(packed_rows(w1, w2, w3, n_lat))
    half = rows // (2 * TAIL) * TAIL
    bounds = ((0, half), (half, rows))
    return pl.pallas_call(
        functools.partial(pack_kernel, n_lat, bounds),
        out_shape=[jax.ShapeDtypeStruct((b - a, width), BF16) for a, b in bounds],
        in_specs=[SMEM, ANY, ANY, ANY, VMEM],
        out_specs=[VMEM] * len(bounds),
        scratch_shapes=[pltpu.SemaphoreType.DMA((16,))],
        name="pack",
    )(pos, w1, w2, w3, scale)


def spread_weights(packed, group, n_lon, n_lat):
    found = {0: packed}
    bits = sorted(bits_down(n_lon // group))
    for bit in bits:
        found[bit] = tuple(exchange(a, "lon", bit * group) for a in packed)
    for far in range(n_lon // group):
        if far not in found:
            bottom = far & -far
            found[far] = tuple(exchange(a, "lon", bottom * group) for a in found[far ^ bottom])
    gathered = {}
    for served in sorted(found):
        if served == 0:
            continue
        parts = {0: found[served]}
        nearest = served & -served
        for bit in bits_down(n_lat):
            for near in list(parts):
                *early, last = parts[near]
                chunks = [exchange(a, "lat", bit) for a in early]
                if near == 0 and bit == n_lat // 2 and served != nearest:
                    joined = gathered[served ^ nearest][bit][-1]
                    chunks.append(exchange(joined, "lon", nearest * group))
                else:
                    chunks.append(exchange(last, "lat", bit))
                parts[near | bit] = tuple(chunks)
        gathered[served] = parts
    return gathered


def radiance_kernel(group, pos, table, source, *outs):
    slots, served, span, _ = outs[0].shape
    for c, out in enumerate(outs, 1):
        for s in range(slots):
            for w in range(served):
                block = table[s, pos[0] ^ (w * group + c)]
                out[s, w] = source[s, pl.ds(pl.multiple_of(block * span, span), span)]


def send_radiances(pos, table, radiances, group, served, span):
    slots, _, channels = radiances.shape
    shape = jax.ShapeDtypeStruct((slots, served, span, channels), BF16)
    return pl.pallas_call(
        functools.partial(radiance_kernel, group),
        out_shape=[shape] * (group - 1),
        in_specs=[SMEM, SMEM, VMEM],
        out_specs=[VMEM] * (group - 1),
        name="pick_radiances",
    )(pos, table, radiances)


def vertical_sum(values):
    lane = lax.broadcasted_iota(jnp.int32, values.shape, 1)
    size = values.shape[1]
    upper = jnp.where(lane == size - 1, 0.0, pltpu.roll(values, size - 1, 1))
    lower = jnp.where(lane == 0, 0.0, pltpu.roll(values, 1, 1))
    return upper + lower


def step_value(centre, east, west, north, south, zonal, meridional, kappa):
    transport = 0.5 * ADVECTION * (zonal * (east - west) + meridional * (north - south))
    spread = east + west + north + south - 4.0 * centre
    return centre - transport + kappa * spread + VERTICAL * (vertical_sum(centre) - 2.0 * centre)


def forward_kernel(group, pos, table, state, kappa, south, north, west, east, wide, first, columns, *sends):
    rows, fields, width, levels = state.shape
    inner = pl.ds(EDGE, width)

    def place(r, _):
        wide[r + 2, 0:fields, inner] = state[r]
        wide[r + 2, fields, inner] = kappa[r]
        return 0

    lax.fori_loop(0, rows, place, 0)
    for r in range(2):
        for target, source in ((r, south), (rows + 2 + r, north)):
            wide[target, :, inner] = source[r, :, 0:width]
            wide[target, :, EDGE - 2 : EDGE] = source[r, :, width : width + 2]
            wide[target, :, EDGE + width : EDGE + width + 2] = source[r, :, width + 2 : width + 4]

    def rims(r, _):
        wide[r + 2, :, EDGE - 2 : EDGE] = west[r]
        wide[r + 2, :, EDGE + width : EDGE + width + 2] = east[r]
        return 0

    lax.fori_loop(0, rows, rims, 0)
    low = EDGE - SIDE
    span = width + 2 * SIDE

    def first_row(r, _):
        zonal = wide[r + 1, 0, pl.ds(low, span)]
        meridional = wide[r + 1, 1, pl.ds(low, span)]
        k = wide[r + 1, fields, pl.ds(low, span)]
        for f in range(fields):
            first[r, f] = step_value(
                wide[r + 1, f, pl.ds(low, span)],
                wide[r + 1, f, pl.ds(low + 1, span)],
                wide[r + 1, f, pl.ds(low - 1, span)],
                wide[r + 2, f, pl.ds(low, span)],
                wide[r, f, pl.ds(low, span)],
                zonal,
                meridional,
                k,
            )
        return 0

    lax.fori_loop(0, rows + 2, first_row, 0)

    def second_row(r, _):
        here = pl.ds(SIDE, width)
        zonal = first[r + 1, 0, here]
        meridional = first[r + 1, 1, here]
        k = wide[r + 2, fields, inner]
        lines = pl.ds(pl.multiple_of(r * width, width), width)
        for f in range(fields):
            centre = first[r + 1, f, here]
            value = step_value(
                centre,
                first[r + 1, f, pl.ds(SIDE + 1, width)],
                first[r + 1, f, pl.ds(SIDE - 1, width)],
                first[r + 2, f, here],
                first[r, f, here],
                zonal,
                meridional,
                k,
            )
            columns[0, lines, f * levels : (f + 1) * levels] = centre.astype(BF16)
            columns[1, lines, f * levels : (f + 1) * levels] = value.astype(BF16)
        return 0

    lax.fori_loop(0, rows, second_row, 0)
    slots, served, block, _ = sends[0].shape
    for c, send in enumerate(sends, 1):
        for s in range(slots):
            for w in range(served):
                b = table[s, pos[0] ^ (w * group + c)]
                send[s, w] = columns[s, pl.ds(pl.multiple_of(b * block, block), block)]


def forward(pos, table, state, kappa, rims, group, served, block):
    rows, fields, width, levels = state.shape
    slots = table.shape[0]
    outs = [
        jax.ShapeDtypeStruct((rows + 4, fields + 1, width + 2 * EDGE, levels), F32),
        jax.ShapeDtypeStruct((rows + 2, fields, width + 2 * SIDE, levels), F32),
        jax.ShapeDtypeStruct((slots, rows * width, fields * levels), BF16),
    ] + [jax.ShapeDtypeStruct((slots, served, block, fields * levels), BF16)] * (group - 1)
    return pl.pallas_call(
        functools.partial(forward_kernel, group),
        out_shape=outs,
        in_specs=[SMEM, SMEM] + [VMEM] * 6,
        out_specs=[VMEM] * len(outs),
        compiler_params=params(16),
        name="forward",
    )(pos, table, state, kappa, *rims)


def halo_of_state(state, kappa):
    width = state.shape[2]

    def cut(rows, columns):
        return jnp.concatenate([state[rows, :, columns], kappa[rows, None, columns]], axis=1)

    every = slice(None)
    west = shifted(cut(every, slice(width - 2, width)), "lon", 1, True)
    east = shifted(cut(every, slice(0, 2)), "lon", -1, True)

    def edge(rows):
        return jnp.concatenate([cut(rows, every), west[rows], east[rows]], axis=2)

    south = shifted(edge(slice(-2, None)), "lat", 1, False)
    north = shifted(edge(slice(0, 2)), "lat", -1, False)
    return south, north, west, east


def backward_kernel(first_half, *refs):
    if first_half:
        adj, south, north, west, east, base, kappa, extra, out, lo, hi, we, ea, pad = refs
        shift, row0 = SIDE, 0
    else:
        adj, south, north, west, east, base, extra, other, out, pad = refs
        shift, row0 = EDGE, 1
    rows, fields, width, levels = adj.shape
    inner = pl.ds(EDGE, width)

    def place(r, _):
        pad[r + 1, :, inner] = adj[r].astype(F32)
        pad[r + 1, :, EDGE - 1 : EDGE] = west[r][:, None]
        pad[r + 1, :, EDGE + width : EDGE + width + 1] = east[r][:, None]
        return 0

    lax.fori_loop(0, rows, place, 0)
    pad[0, :, inner] = south[...].astype(F32)
    pad[rows + 1, :, inner] = north[...].astype(F32)
    half = 0.5 * ADVECTION

    def diffusion(r, at):
        if first_half:
            return kappa[r + 1, 0, pl.ds(EDGE + at, width)]
        return base[r + 1, fields, pl.ds(EDGE + at, width)]

    def wind(r, f, at):
        return base[r + row0, f, pl.ds(shift + at, width)]

    def row(r, _):
        c_here = (1.0 - 2.0 * VERTICAL) - 4.0 * diffusion(r + 1, 0)
        c_west = diffusion(r + 1, -1) - half * wind(r + 1, 0, -1)
        c_east = diffusion(r + 1, 1) + half * wind(r + 1, 0, 1)
        c_south = diffusion(r, 0) - half * wind(r, 1, 0)
        c_north = diffusion(r + 2, 0) + half * wind(r + 2, 1, 0)
        zonal = jnp.zeros((width, levels), F32)
        meridional = jnp.zeros((width, levels), F32)
        for f in range(fields):
            here = pad[r + 1, f, inner]
            zonal += here * (wind(r + 1, f, 1) - wind(r + 1, f, -1))
            meridional += here * (wind(r + 2, f, 0) - wind(r, f, 0))
        for f in range(fields):
            here = pad[r + 1, f, inner]
            value = (
                here * c_here
                + pad[r + 1, f, pl.ds(EDGE - 1, width)] * c_west
                + pad[r + 1, f, pl.ds(EDGE + 1, width)] * c_east
                + pad[r, f, inner] * c_south
                + pad[r + 2, f, inner] * c_north
                + VERTICAL * vertical_sum(here)
            )
            if f == 0:
                value -= half * zonal
            if f == 1:
                value -= half * meridional
            if first_half:
                value += extra[r, f].astype(F32)
                we[r, f : f + 1] = value[0:1]
                ea[r, f : f + 1] = value[width - 1 : width]
            else:
                value += extra[r, f] - other[r, f]
            out[r, f] = value
        return 0

    lax.fori_loop(0, rows, row, 0)
    if first_half:
        lo[...] = out[0]
        hi[...] = out[rows - 1]


def halo_of_adjoint(edges):
    low, high, west, east = edges
    return (
        shifted(high, "lat", 1, False),
        shifted(low, "lat", -1, False),
        shifted(east, "lon", 1, True),
        shifted(west, "lon", -1, True),
    )


def backward_first(adjoint, rims, first, wide, forcing):
    rows, fields, width, levels = adjoint.shape
    line = jax.ShapeDtypeStruct((fields, width, levels), F32)
    side = jax.ShapeDtypeStruct((rows, fields, levels), F32)
    kappa_spec = pl.BlockSpec(
        (rows + 4, 1, width + 2 * EDGE, levels), lambda i: (0, fields, 0, 0)
    )

    def whole(shape):
        return pl.BlockSpec(shape, lambda i: (0,) * len(shape))

    out, *edges = pl.pallas_call(
        functools.partial(backward_kernel, True),
        grid=(1,),
        out_shape=[jax.ShapeDtypeStruct(adjoint.shape, F32), line, line, side, side],
        in_specs=[whole(a.shape) for a in (adjoint, *rims, first)]
        + [kappa_spec, whole(forcing.shape)],
        out_specs=[whole(adjoint.shape), whole(line.shape), whole(line.shape), whole(side.shape), whole(side.shape)],
        scratch_shapes=[pltpu.VMEM((rows + 2, fields, width + 2 * EDGE, levels), F32)],
        compiler_params=params(16),
        name="backward_first",
    )(adjoint, *rims, first, wide, forcing)
    return out, edges


def backward_last(adjoint, rims, wide, state, background):
    rows, fields, width, levels = adjoint.shape
    return pl.pallas_call(
        functools.partial(backward_kernel, False),
        out_shape=jax.ShapeDtypeStruct(adjoint.shape, F32),
        in_specs=[VMEM] * 8,
        out_specs=VMEM,
        scratch_shapes=[pltpu.VMEM((rows + 2, fields, width + 2 * EDGE, levels), F32)],
        compiler_params=params(16),
        name="backward_last",
    )(adjoint, *rims, wide, state, background)


def nt_dot(a, b):
    return lax.dot_general(a, b, (((1,), (1,)), ((), ())), preferred_element_type=F32)


def instrument_kernel(group, served, n_lat, chosen, bounds, pos, table, columns, radiances, *refs):
    others = group - 1
    got_columns, refs = refs[:others], refs[others:]
    got_radiances, refs = refs[:others], refs[others:]
    own_weights = served == 0
    n_weights = 4 if own_weights else n_lat * len(bounds)
    weights, refs = refs[:n_weights], refs[n_weights:]
    outs, refs = refs[:group], refs[group:]
    x, y, a1, s1, a2, s2, mis, *built = refs
    slots, span, _ = outs[0].shape
    tile = 256
    for c in range(group):
        for k, s in enumerate(chosen):
            j = c * slots + k
            lines = slice(j * span, (j + 1) * span)
            if c == 0:
                block = table[s, pos[0] ^ (served * group)]
                at = pl.ds(pl.multiple_of(block * span, span), span)
                x[lines] = columns[s, at]
                y[lines] = radiances[s, at]
            else:
                x[lines] = got_columns[c - 1][s, served]
                y[lines] = got_radiances[c - 1][s, served]
    if own_weights:
        w1, w2, w3, scale = weights
        factor = scale[...]
    else:
        w1, w2, w3 = built
        r1, r2, piece, _ = packed_rows(w1, w2, w3, n_lat)
        parts = w2.shape[1] // w3.shape[1]
        ends = (r1, r1 + r2, r1 + r2 + piece)
        everything = pl.ds(0, w1.shape[1])

        def fetch(first, last, lanes, target, base):
            for source, onto in fetches(sources, bounds, first, last, lanes, target, base):
                onto[...] = source[...]

        for near in range(n_lat):
            lat = pos[1] ^ near
            sources = weights[near * len(bounds) : (near + 1) * len(bounds)]
            fetch(0, ends[0], everything, w1, lat * r1)
            fetch(ends[0], ends[1], everything, w2, lat * r2)
            for p in range(parts):
                fetch(ends[1], ends[2], pl.ds(p * w3.shape[1], w3.shape[1]), w3, (lat * parts + p) * piece)
        last, low = weights[len(bounds) - 1], bounds[-1][0]
        triple = last[ends[2] - low : ends[2] - low + TAIL, 0 : w3.shape[1]].astype(F32)
        factor = triple[0:1] + triple[1:2] + triple[2:3]

    def hidden(source, weight, act, slope):
        def column(n, _):
            at = pl.ds(pl.multiple_of(n * tile, tile), tile)
            z = jnp.dot(source[...], weight[:, at], preferred_element_type=F32)
            half = 0.5 * jnp.tanh(0.5 * z)
            sigma = 0.5 + half
            value = z * sigma
            act[:, at] = value.astype(BF16)
            slope[:, at] = sigma + value * (0.5 - half)
            return 0

        lax.fori_loop(0, weight.shape[1] // tile, column, 0, unroll=True)

    hidden(x, w1, a1, s1)
    hidden(a1, w2, a2, s2)
    for n in range(w3.shape[1] // tile):
        at = slice(n * tile, (n + 1) * tile)
        evolved = jnp.dot(a2[...], w3[:, at], preferred_element_type=F32)
        mis[:, at] = (factor[:, at] * (evolved - y[:, at].astype(F32))).astype(BF16)

    def back(source, weight, slope, grad):
        def column(n, _):
            at = pl.ds(pl.multiple_of(n * tile, tile), tile)
            grad[:, at] = (nt_dot(source[...], weight[at]) * slope[:, at]).astype(BF16)
            return 0

        lax.fori_loop(0, weight.shape[0] // tile, column, 0, unroll=True)

    back(mis, w3, s2, a2)
    back(a2, w2, s1, a1)
    for n in range(w1.shape[0] // tile):
        at = slice(n * tile, (n + 1) * tile)
        value = nt_dot(a1[...], w1[at]).astype(BF16)
        for j in range(group * slots):
            outs[j // slots][j % slots, :, at] = value[j * span : (j + 1) * span]


def instrument(pos, table, columns, radiances, got_columns, got_radiances, weights, group, served, n_lat, sizes, span, chosen):
    cin, ch = columns.shape[2], radiances.shape[2]
    slots = len(chosen)
    h1, h2 = sizes
    own = served == 0
    bounds = []
    if not own:
        for chunk in weights[0]:
            low = bounds[-1][1] if bounds else 0
            bounds.append((low, low + chunk.shape[0]))
        weights = [chunk for near in range(n_lat) for chunk in weights[near]]
    lines = group * slots * span
    out = jax.ShapeDtypeStruct((slots, span, cin), BF16)
    return pl.pallas_call(
        functools.partial(instrument_kernel, group, served, n_lat, chosen, tuple(bounds)),
        out_shape=[out] * group,
        in_specs=[SMEM, SMEM] + [VMEM] * (2 + 2 * (group - 1) + len(weights)),
        out_specs=[VMEM] * group,
        scratch_shapes=[
            pltpu.VMEM((lines, cin), BF16),
            pltpu.VMEM((lines, ch), BF16),
            pltpu.VMEM((lines, h1), BF16),
            pltpu.VMEM((lines, h1), F32),
            pltpu.VMEM((lines, h2), BF16),
            pltpu.VMEM((lines, h2), F32),
            pltpu.VMEM((lines, ch), BF16),
        ]
        + ([] if own else [pltpu.VMEM(shape, BF16) for shape in ((cin, h1), (h1, h2), (h2, ch))]),
        compiler_params=params(20),
        cost_estimate=pl.CostEstimate(
            flops=4 * lines * (cin * h1 + h1 * h2 + h2 * ch),
            transcendentals=lines * (h1 + h2),
            bytes_accessed=2 * (cin * h1 + h1 * h2 + h2 * ch + lines * (2 * cin + ch)),
        ),
    )(pos, table, columns, radiances, *got_columns, *got_radiances, *weights)


def collect_kernel(slot, places, edges, pos, owners, *refs):
    outs = 5 if edges else 1
    *answers, flat = refs[: len(refs) - 1 - outs] + refs[len(refs) - 1 :]
    out, *rims = refs[len(answers) : len(answers) + outs]
    rows, fields, width, levels = out.shape
    span = answers[0].shape[1]

    def block(b, _):
        apart = owners[slot, b] ^ pos[0]
        for k, answer in enumerate(answers):

            @pl.when(apart == k)
            def _():
                flat[pl.ds(pl.multiple_of(b * span, span), span)] = answer[places[k]]

        return 0

    lax.fori_loop(0, rows * width // span, block, 0)

    def row(r, _):
        lines = pl.ds(pl.multiple_of(r * width, width), width)
        for f in range(fields):
            value = flat[lines, f * levels : (f + 1) * levels]
            out[r, f] = value
            if edges:
                wide = value.astype(F32)
                rims[2][r, f : f + 1] = wide[0:1]
                rims[3][r, f : f + 1] = wide[width - 1 : width]
        return 0

    lax.fori_loop(0, rows, row, 0)
    if edges:
        rims[0][...] = out[0]
        rims[1][...] = out[rows - 1]


def collect(slot, pos, owners, answers, shape, edges):
    places = tuple(place for _, place in answers)
    answers = [answer for answer, _ in answers]
    rows, fields, width, levels = shape
    outs = [jax.ShapeDtypeStruct(shape, BF16)]
    if edges:
        outs += [jax.ShapeDtypeStruct((fields, width, levels), BF16)] * 2
        outs += [jax.ShapeDtypeStruct((rows, fields, levels), F32)] * 2
    return pl.pallas_call(
        functools.partial(collect_kernel, slot, places, edges),
        out_shape=outs,
        in_specs=[SMEM, SMEM] + [VMEM] * len(answers),
        out_specs=[VMEM] * len(outs),
        scratch_shapes=[pltpu.VMEM((rows * width, fields * levels), BF16)],
        compiler_params=params(16),
    )(pos, owners, *answers)


def shards(state, background, diffusivity, radiances, owners, first_layer, second_layer, third_layer, channel_weight):
    n_lon, n_lat = lax.axis_size("lon"), lax.axis_size("lat")
    served = min(SERVED, n_lon)
    group = n_lon // served
    slots, _, blocks = owners.shape
    rows, width, _, _ = state.shape
    span = rows * width // blocks
    h1, h2 = first_layer.shape[2], second_layer.shape[2]
    pos = jnp.stack([lax.axis_index("lon"), lax.axis_index("lat")]).astype(jnp.int32)
    owners = owners[:, 0]
    hits = owners[:, None, :] == jnp.arange(n_lon, dtype=jnp.int32)[None, :, None]
    table = jnp.sum(jnp.where(hits, jnp.arange(blocks, dtype=jnp.int32), 0), axis=2)
    state = state.transpose(0, 2, 1, 3)
    background = background.transpose(0, 2, 1, 3)
    radiances = radiances.reshape(slots, rows * width, -1)
    own = (first_layer[0], second_layer[0], third_layer[0], channel_weight)

    rims = halo_of_state(state, diffusivity)
    gathered = spread_weights(pack_weights(pos, own, n_lat), group, n_lon, n_lat)
    sent = send_radiances(pos, table, radiances, group, served, span)
    got_radiances = [exchange(a, "lon", c) for c, a in enumerate(sent, 1)]
    wide, first, columns, *sent = forward(pos, table, state, diffusivity, rims, group, served, span)
    got_columns = [exchange(a, "lon", c) for c, a in enumerate(sent, 1)]

    answers = {s: [] for s in range(slots)}
    for w in range(served):
        weights = own if w == 0 else [gathered[w][k] for k in range(n_lat)]
        for chosen in [(s,) for s in reversed(range(slots))] if w == served - 1 else [tuple(range(slots))]:
            mine, *theirs = instrument(
                pos, table, columns, radiances, got_columns, got_radiances, weights, group, w, n_lat, (h1, h2), span, chosen
            )
            back = [exchange(a, "lon", c) for c, a in enumerate(theirs, 1)]
            for place, s in enumerate(chosen):
                answers[s] += [(mine, place)] + [(a, place) for a in back]
    shape = state.shape
    late, *edges = collect(1, pos, owners, answers[1], shape, True)
    (early,) = collect(0, pos, owners, answers[0], shape, False)
    costate, edges = backward_first(late, halo_of_adjoint(edges), first, wide, early)
    gradient = backward_last(costate, halo_of_adjoint(edges), wide, state, background)
    return gradient.transpose(0, 2, 1, 3)


def solution(mesh):
    placed = (
        P("lat", "lon", None, None),
        P("lat", "lon", None, None),
        P("lat", "lon", None),
        P(None, "lat", "lon", None),
        P(None, "lat", "lon"),
        P("lon", None, None),
        P("lon", None, None),
        P("lon", None, None),
        P("lon", None),
    )
    return jax.shard_map(shards, mesh=mesh, in_specs=placed, out_specs=P("lat", "lon", None, None), check_vma=False)
```

```python
import functools
import jax
import jax.numpy as jnp
from jax import lax
from jax.experimental import pallas as pl
from jax.experimental.pallas import tpu as pltpu
from jax.sharding import PartitionSpec as P


ADVECTION = 0.25
VERTICAL = 0.1
SERVED = 4
EDGE = 16
SIDE = 8
TAIL = 16
ANY = pl.BlockSpec(memory_space=pl.ANY)
SMEM = pl.BlockSpec(memory_space=pltpu.SMEM)
VMEM = pl.BlockSpec(memory_space=pltpu.VMEM)
F32 = jnp.float32
BF16 = jnp.bfloat16


def params(mib):
    return pltpu.CompilerParams(vmem_limit_bytes=mib << 20)


def exchange(array, axis, mask):
    count = lax.axis_size(axis)
    return lax.ppermute(array, axis, [(i, i ^ mask) for i in range(count)])


def shifted(array, axis, step, periodic):
    count = lax.axis_size(axis)
    pairs = [(i, (i + step) % count) for i in range(count)]
    if not periodic:
        pairs = [(i, j) for i, j in pairs if j == i + step]
    return lax.ppermute(array, axis, pairs)


def paired(array, axis, start, periodic):
    count = lax.axis_size(axis)
    pairs = []
    for i in range(start, count if periodic else count - 1, 2):
        pairs += [(i, (i + 1) % count), ((i + 1) % count, i)]
    return lax.ppermute(array, axis, pairs)


def bits_down(size):
    bit = size // 2
    while bit:
        yield bit
        bit //= 2


def packed_rows(w1, w2, w3, n_lat):
    return (w1.shape[0] // n_lat, w2.shape[0] // n_lat, w3.shape[0] * w3.shape[1] // (w2.shape[1] * n_lat), TAIL)


def fetches(sources, bounds, first, last, lanes, target, base):
    for source, (low, high) in zip(sources, bounds):
        a, b = max(first, low), min(last, high)
        if a < b:
            begin = base + (a - first)
            if not isinstance(begin, int):
                begin = pl.multiple_of(begin, 16)
            yield source.at[pl.ds(a - low, b - a), lanes], target.at[pl.ds(begin, b - a)]


def pack_kernel(n_lat, bounds, pos, w1, w2, w3, scale, *refs):
    *outs, sems = refs
    lat = pos[1]
    width = outs[0].shape[1]
    r1, r2, piece, _ = packed_rows(w1, w2, w3, n_lat)
    parts = width // w3.shape[1]
    ends = (r1, r1 + r2, r1 + r2 + piece, r1 + r2 + piece + TAIL)
    copies = []

    def put(first, last, lanes, source, base):
        for at, onto in fetches(outs, bounds, first, last, lanes, source, base):
            copies.append(pltpu.make_async_copy(onto, at, sems.at[len(copies)]))

    everything = pl.ds(0, width)
    put(0, ends[0], everything, w1, lat * r1)
    put(ends[0], ends[1], everything, w2, lat * r2)
    for j in range(parts):
        put(ends[1], ends[2], pl.ds(j * w3.shape[1], w3.shape[1]), w3, (lat * parts + j) * piece)
    for copy in copies:
        copy.start()
    whole = scale[...]
    high = whole.astype(BF16).astype(F32)
    rest = whole - high
    middle = rest.astype(BF16).astype(F32)
    low = rest - middle
    rows = lax.broadcasted_iota(jnp.int32, (TAIL, scale.shape[1]), 0)
    stacked = jnp.where(rows == 0, high, jnp.where(rows == 1, middle, low))
    for out, (low_row, high_row) in zip(outs, bounds):
        if high_row == ends[3]:
            tail = slice(ends[2] - low_row, ends[3] - low_row)
            out[tail] = jnp.zeros((TAIL, width), BF16)
            out[tail, 0 : scale.shape[1]] = jnp.where(rows < 3, stacked, 0.0).astype(BF16)
    for copy in copies:
        copy.wait()


def pack_weights(pos, weights, n_lat):
    w1, w2, w3, scale = weights
    width = w1.shape[1]
    rows = sum(packed_rows(w1, w2, w3, n_lat))
    half = rows // (2 * TAIL) * TAIL
    bounds = ((0, half), (half, rows))
    return pl.pallas_call(
        functools.partial(pack_kernel, n_lat, bounds),
        out_shape=[jax.ShapeDtypeStruct((b - a, width), BF16) for a, b in bounds],
        in_specs=[SMEM, ANY, ANY, ANY, VMEM],
        out_specs=[VMEM] * len(bounds),
        scratch_shapes=[pltpu.SemaphoreType.DMA((16,))],
        name="pack",
    )(pos, w1, w2, w3, scale)


def spread_weights(packed, group, n_lon, n_lat):
    found = {0: packed}
    bits = sorted(bits_down(n_lon // group))
    for bit in bits:
        found[bit] = tuple(exchange(a, "lon", bit * group) for a in packed)
    for far in range(n_lon // group):
        if far not in found:
            bottom = far & -far
            found[far] = tuple(exchange(a, "lon", bottom * group) for a in found[far ^ bottom])
    gathered = {}
    for served in sorted(found):
        if served == 0:
            continue
        parts = {0: found[served]}
        nearest = served & -served
        for bit in bits_down(n_lat):
            for near in list(parts):
                *early, last = parts[near]
                chunks = [exchange(a, "lat", bit) for a in early]
                if near == 0 and bit == n_lat // 2 and served != nearest:
                    joined = gathered[served ^ nearest][bit][-1]
                    chunks.append(exchange(joined, "lon", nearest * group))
                else:
                    chunks.append(exchange(last, "lat", bit))
                parts[near | bit] = tuple(chunks)
        gathered[served] = parts
    return gathered


def radiance_kernel(group, pos, table, source, *outs):
    slots, served, span, _ = outs[0].shape
    for c, out in enumerate(outs, 1):
        for s in range(slots):
            for w in range(served):
                block = table[s, pos[0] ^ (w * group + c)]
                out[s, w] = source[s, pl.ds(pl.multiple_of(block * span, span), span)]


def send_radiances(pos, table, radiances, group, served, span):
    slots, _, channels = radiances.shape
    shape = jax.ShapeDtypeStruct((slots, served, span, channels), BF16)
    return pl.pallas_call(
        functools.partial(radiance_kernel, group),
        out_shape=[shape] * (group - 1),
        in_specs=[SMEM, SMEM, VMEM],
        out_specs=[VMEM] * (group - 1),
        name="pick_radiances",
    )(pos, table, radiances)


def vertical_sum(values):
    lane = lax.broadcasted_iota(jnp.int32, values.shape, 1)
    size = values.shape[1]
    upper = jnp.where(lane == size - 1, 0.0, pltpu.roll(values, size - 1, 1))
    lower = jnp.where(lane == 0, 0.0, pltpu.roll(values, 1, 1))
    return upper + lower


def step_value(centre, east, west, north, south, zonal, meridional, kappa):
    transport = 0.5 * ADVECTION * (zonal * (east - west) + meridional * (north - south))
    spread = east + west + north + south - 4.0 * centre
    return centre - transport + kappa * spread + VERTICAL * (vertical_sum(centre) - 2.0 * centre)


def forward_kernel(group, pos, table, state, kappa, south, north, west, east, wide, first, columns, *sends):
    rows, fields, width, levels = state.shape
    inner = pl.ds(EDGE, width)

    def place(r, _):
        wide[r + 2, 0:fields, inner] = state[r]
        wide[r + 2, fields, inner] = kappa[r]
        return 0

    lax.fori_loop(0, rows, place, 0)
    for r in range(2):
        for target, source in ((r, south), (rows + 2 + r, north)):
            wide[target, :, inner] = source[r, :, 0:width]
            wide[target, :, EDGE - 2 : EDGE] = source[r, :, width : width + 2]
            wide[target, :, EDGE + width : EDGE + width + 2] = source[r, :, width + 2 : width + 4]

    def rims(r, _):
        wide[r + 2, :, EDGE - 2 : EDGE] = west[r]
        wide[r + 2, :, EDGE + width : EDGE + width + 2] = east[r]
        return 0

    lax.fori_loop(0, rows, rims, 0)
    low = EDGE - SIDE
    span = width + 2 * SIDE

    def first_row(r, _):
        zonal = wide[r + 1, 0, pl.ds(low, span)]
        meridional = wide[r + 1, 1, pl.ds(low, span)]
        k = wide[r + 1, fields, pl.ds(low, span)]
        for f in range(fields):
            first[r, f] = step_value(
                wide[r + 1, f, pl.ds(low, span)],
                wide[r + 1, f, pl.ds(low + 1, span)],
                wide[r + 1, f, pl.ds(low - 1, span)],
                wide[r + 2, f, pl.ds(low, span)],
                wide[r, f, pl.ds(low, span)],
                zonal,
                meridional,
                k,
            )
        return 0

    lax.fori_loop(0, rows + 2, first_row, 0)

    def second_row(r, _):
        here = pl.ds(SIDE, width)
        zonal = first[r + 1, 0, here]
        meridional = first[r + 1, 1, here]
        k = wide[r + 2, fields, inner]
        lines = pl.ds(pl.multiple_of(r * width, width), width)
        for f in range(fields):
            centre = first[r + 1, f, here]
            value = step_value(
                centre,
                first[r + 1, f, pl.ds(SIDE + 1, width)],
                first[r + 1, f, pl.ds(SIDE - 1, width)],
                first[r + 2, f, here],
                first[r, f, here],
                zonal,
                meridional,
                k,
            )
            columns[0, lines, f * levels : (f + 1) * levels] = centre.astype(BF16)
            columns[1, lines, f * levels : (f + 1) * levels] = value.astype(BF16)
        return 0

    lax.fori_loop(0, rows, second_row, 0)
    slots, served, block, _ = sends[0].shape
    for c, send in enumerate(sends, 1):
        for s in range(slots):
            for w in range(served):
                b = table[s, pos[0] ^ (w * group + c)]
                send[s, w] = columns[s, pl.ds(pl.multiple_of(b * block, block), block)]


def forward(pos, table, state, kappa, rims, group, served, block):
    rows, fields, width, levels = state.shape
    slots = table.shape[0]
    outs = [
        jax.ShapeDtypeStruct((rows + 4, fields + 1, width + 2 * EDGE, levels), F32),
        jax.ShapeDtypeStruct((rows + 2, fields, width + 2 * SIDE, levels), F32),
        jax.ShapeDtypeStruct((slots, rows * width, fields * levels), BF16),
    ] + [jax.ShapeDtypeStruct((slots, served, block, fields * levels), BF16)] * (group - 1)
    return pl.pallas_call(
        functools.partial(forward_kernel, group),
        out_shape=outs,
        in_specs=[SMEM, SMEM] + [VMEM] * 6,
        out_specs=[VMEM] * len(outs),
        compiler_params=params(16),
        name="forward",
    )(pos, table, state, kappa, *rims)


def halo_of_state(state, kappa):
    width = state.shape[2]

    def cut(rows, columns):
        return jnp.concatenate([state[rows, :, columns], kappa[rows, None, columns]], axis=1)

    every = slice(None)
    west = shifted(cut(every, slice(width - 2, width)), "lon", 1, True)
    east = shifted(cut(every, slice(0, 2)), "lon", -1, True)

    def edge(rows):
        return jnp.concatenate([cut(rows, every), west[rows], east[rows]], axis=2)

    south = shifted(edge(slice(-2, None)), "lat", 1, False)
    north = shifted(edge(slice(0, 2)), "lat", -1, False)
    return south, north, west, east


def backward_kernel(first_half, *refs):
    if first_half:
        pos, adj, inner_row, outer_row, close, distant, base, kappa, extra, out, lo, hi, we, ea, pad = refs
        shift, row0 = SIDE, 0
    else:
        pos, adj, inner_row, outer_row, close, distant, base, extra, other, out, pad = refs
        shift, row0 = EDGE, 1
    rows, fields, width, levels = adj.shape
    inner = pl.ds(EDGE, width)
    even_lon = pos[0] % 2 == 0

    def place(r, _):
        pad[r + 1, :, inner] = adj[r].astype(F32)
        one, two = close[r], distant[r]
        pad[r + 1, :, EDGE - 1 : EDGE] = jnp.where(even_lon, two, one)[:, None]
        pad[r + 1, :, EDGE + width : EDGE + width + 1] = jnp.where(even_lon, one, two)[:, None]
        return 0

    lax.fori_loop(0, rows, place, 0)
    even = pos[1] % 2 == 0
    pad[jnp.where(even, rows + 1, 0), :, inner] = inner_row[...].astype(F32)
    pad[jnp.where(even, 0, rows + 1), :, inner] = outer_row[...].astype(F32)
    half = 0.5 * ADVECTION

    def diffusion(r, at):
        if first_half:
            return kappa[r + 1, 0, pl.ds(EDGE + at, width)]
        return base[r + 1, fields, pl.ds(EDGE + at, width)]

    def wind(r, f, at):
        return base[r + row0, f, pl.ds(shift + at, width)]

    def row(r, _):
        c_here = (1.0 - 2.0 * VERTICAL) - 4.0 * diffusion(r + 1, 0)
        c_west = diffusion(r + 1, -1) - half * wind(r + 1, 0, -1)
        c_east = diffusion(r + 1, 1) + half * wind(r + 1, 0, 1)
        c_south = diffusion(r, 0) - half * wind(r, 1, 0)
        c_north = diffusion(r + 2, 0) + half * wind(r + 2, 1, 0)
        zonal = jnp.zeros((width, levels), F32)
        meridional = jnp.zeros((width, levels), F32)
        for f in range(fields):
            here = pad[r + 1, f, inner]
            zonal += here * (wind(r + 1, f, 1) - wind(r + 1, f, -1))
            meridional += here * (wind(r + 2, f, 0) - wind(r, f, 0))
        for f in range(fields):
            here = pad[r + 1, f, inner]
            value = (
                here * c_here
                + pad[r + 1, f, pl.ds(EDGE - 1, width)] * c_west
                + pad[r + 1, f, pl.ds(EDGE + 1, width)] * c_east
                + pad[r, f, inner] * c_south
                + pad[r + 2, f, inner] * c_north
                + VERTICAL * vertical_sum(here)
            )
            if f == 0:
                value -= half * zonal
            if f == 1:
                value -= half * meridional
            if first_half:
                value += extra[r, f].astype(F32)
                begin, end = value[0:1], value[width - 1 : width]
                we[r, f : f + 1] = jnp.where(even_lon, end, begin)
                ea[r, f : f + 1] = jnp.where(even_lon, begin, end)
            else:
                value += extra[r, f] - other[r, f]
            out[r, f] = value
        return 0

    lax.fori_loop(0, rows, row, 0)
    if first_half:
        lo[...] = out[jnp.where(even, rows - 1, 0)]
        hi[...] = out[jnp.where(even, 0, rows - 1)]


def halo_of_adjoint(edges):
    inner, outer, close, distant = edges
    return (
        paired(inner, "lat", 0, False),
        paired(outer, "lat", 1, False),
        paired(close, "lon", 0, True),
        paired(distant, "lon", 1, True),
    )


def backward_first(pos, adjoint, rims, first, wide, forcing):
    rows, fields, width, levels = adjoint.shape
    line = jax.ShapeDtypeStruct((fields, width, levels), F32)
    side = jax.ShapeDtypeStruct((rows, fields, levels), F32)
    kappa_spec = pl.BlockSpec(
        (rows + 4, 1, width + 2 * EDGE, levels), lambda i: (0, fields, 0, 0)
    )

    def whole(shape):
        return pl.BlockSpec(shape, lambda i: (0,) * len(shape))

    out, *edges = pl.pallas_call(
        functools.partial(backward_kernel, True),
        grid=(1,),
        out_shape=[jax.ShapeDtypeStruct(adjoint.shape, F32), line, line, side, side],
        in_specs=[SMEM]
        + [whole(a.shape) for a in (adjoint, *rims, first)]
        + [kappa_spec, whole(forcing.shape)],
        out_specs=[whole(adjoint.shape), whole(line.shape), whole(line.shape), whole(side.shape), whole(side.shape)],
        scratch_shapes=[pltpu.VMEM((rows + 2, fields, width + 2 * EDGE, levels), F32)],
        compiler_params=params(16),
        name="backward_first",
    )(pos, adjoint, *rims, first, wide, forcing)
    return out, edges


def backward_last(pos, adjoint, rims, wide, state, background):
    rows, fields, width, levels = adjoint.shape
    return pl.pallas_call(
        functools.partial(backward_kernel, False),
        out_shape=jax.ShapeDtypeStruct(adjoint.shape, F32),
        in_specs=[SMEM] + [VMEM] * 8,
        out_specs=VMEM,
        scratch_shapes=[pltpu.VMEM((rows + 2, fields, width + 2 * EDGE, levels), F32)],
        compiler_params=params(16),
        name="backward_last",
    )(pos, adjoint, *rims, wide, state, background)


def nt_dot(a, b):
    return lax.dot_general(a, b, (((1,), (1,)), ((), ())), preferred_element_type=F32)


def instrument_kernel(group, served, n_lat, chosen, bounds, pos, table, columns, radiances, *refs):
    others = group - 1
    got_columns, refs = refs[:others], refs[others:]
    got_radiances, refs = refs[:others], refs[others:]
    own_weights = served == 0
    n_weights = 4 if own_weights else n_lat * len(bounds)
    weights, refs = refs[:n_weights], refs[n_weights:]
    outs, refs = refs[:group], refs[group:]
    x, y, a1, s1, a2, s2, mis, *built = refs
    slots, span, _ = outs[0].shape
    tile = 256
    for c in range(group):
        for k, s in enumerate(chosen):
            j = c * slots + k
            lines = slice(j * span, (j + 1) * span)
            if c == 0:
                block = table[s, pos[0] ^ (served * group)]
                at = pl.ds(pl.multiple_of(block * span, span), span)
                x[lines] = columns[s, at]
                y[lines] = radiances[s, at]
            else:
                x[lines] = got_columns[c - 1][s, served]
                y[lines] = got_radiances[c - 1][s, served]
    if own_weights:
        w1, w2, w3, scale = weights
        factor = scale[...]
    else:
        w1, w2, w3 = built
        r1, r2, piece, _ = packed_rows(w1, w2, w3, n_lat)
        parts = w2.shape[1] // w3.shape[1]
        ends = (r1, r1 + r2, r1 + r2 + piece)
        everything = pl.ds(0, w1.shape[1])

        def fetch(first, last, lanes, target, base):
            for source, onto in fetches(sources, bounds, first, last, lanes, target, base):
                onto[...] = source[...]

        for near in range(n_lat):
            lat = pos[1] ^ near
            sources = weights[near * len(bounds) : (near + 1) * len(bounds)]
            fetch(0, ends[0], everything, w1, lat * r1)
            fetch(ends[0], ends[1], everything, w2, lat * r2)
            for p in range(parts):
                fetch(ends[1], ends[2], pl.ds(p * w3.shape[1], w3.shape[1]), w3, (lat * parts + p) * piece)
        last, low = weights[len(bounds) - 1], bounds[-1][0]
        triple = last[ends[2] - low : ends[2] - low + TAIL, 0 : w3.shape[1]].astype(F32)
        factor = triple[0:1] + triple[1:2] + triple[2:3]

    def hidden(source, weight, act, slope):
        def column(n, _):
            at = pl.ds(pl.multiple_of(n * tile, tile), tile)
            z = jnp.dot(source[...], weight[:, at], preferred_element_type=F32)
            half = 0.5 * jnp.tanh(0.5 * z)
            sigma = 0.5 + half
            value = z * sigma
            act[:, at] = value.astype(BF16)
            slope[:, at] = sigma + value * (0.5 - half)
            return 0

        lax.fori_loop(0, weight.shape[1] // tile, column, 0, unroll=True)

    hidden(x, w1, a1, s1)
    hidden(a1, w2, a2, s2)
    for n in range(w3.shape[1] // tile):
        at = slice(n * tile, (n + 1) * tile)
        evolved = jnp.dot(a2[...], w3[:, at], preferred_element_type=F32)
        mis[:, at] = (factor[:, at] * (evolved - y[:, at].astype(F32))).astype(BF16)

    def back(source, weight, slope, grad):
        def column(n, _):
            at = pl.ds(pl.multiple_of(n * tile, tile), tile)
            grad[:, at] = (nt_dot(source[...], weight[at]) * slope[:, at]).astype(BF16)
            return 0

        lax.fori_loop(0, weight.shape[0] // tile, column, 0, unroll=True)

    back(mis, w3, s2, a2)
    back(a2, w2, s1, a1)
    for n in range(w1.shape[0] // tile):
        at = slice(n * tile, (n + 1) * tile)
        value = nt_dot(a1[...], w1[at]).astype(BF16)
        for j in range(group * slots):
            outs[j // slots][j % slots, :, at] = value[j * span : (j + 1) * span]


def instrument(pos, table, columns, radiances, got_columns, got_radiances, weights, group, served, n_lat, sizes, span, chosen):
    cin, ch = columns.shape[2], radiances.shape[2]
    slots = len(chosen)
    h1, h2 = sizes
    own = served == 0
    bounds = []
    if not own:
        for chunk in weights[0]:
            low = bounds[-1][1] if bounds else 0
            bounds.append((low, low + chunk.shape[0]))
        weights = [chunk for near in range(n_lat) for chunk in weights[near]]
    lines = group * slots * span
    out = jax.ShapeDtypeStruct((slots, span, cin), BF16)
    return pl.pallas_call(
        functools.partial(instrument_kernel, group, served, n_lat, chosen, tuple(bounds)),
        out_shape=[out] * group,
        in_specs=[SMEM, SMEM] + [VMEM] * (2 + 2 * (group - 1) + len(weights)),
        out_specs=[VMEM] * group,
        scratch_shapes=[
            pltpu.VMEM((lines, cin), BF16),
            pltpu.VMEM((lines, ch), BF16),
            pltpu.VMEM((lines, h1), BF16),
            pltpu.VMEM((lines, h1), F32),
            pltpu.VMEM((lines, h2), BF16),
            pltpu.VMEM((lines, h2), F32),
            pltpu.VMEM((lines, ch), BF16),
        ]
        + ([] if own else [pltpu.VMEM(shape, BF16) for shape in ((cin, h1), (h1, h2), (h2, ch))]),
        compiler_params=params(14 + 2 * (group - 1)),
        cost_estimate=pl.CostEstimate(
            flops=4 * lines * (cin * h1 + h1 * h2 + h2 * ch),
            transcendentals=lines * (h1 + h2),
            bytes_accessed=2 * (cin * h1 + h1 * h2 + h2 * ch + lines * (2 * cin + ch)),
        ),
    )(pos, table, columns, radiances, *got_columns, *got_radiances, *weights)


def collect_kernel(slot, places, edges, pos, owners, *refs):
    outs = 5 if edges else 1
    *answers, flat = refs[: len(refs) - 1 - outs] + refs[len(refs) - 1 :]
    out, *rims = refs[len(answers) : len(answers) + outs]
    rows, fields, width, levels = out.shape
    span = answers[0].shape[1]

    def block(b, _):
        apart = owners[slot, b] ^ pos[0]
        for k, answer in enumerate(answers):

            @pl.when(apart == k)
            def _():
                flat[pl.ds(pl.multiple_of(b * span, span), span)] = answer[places[k]]

        return 0

    lax.fori_loop(0, rows * width // span, block, 0)
    even_lon = pos[0] % 2 == 0

    def row(r, _):
        lines = pl.ds(pl.multiple_of(r * width, width), width)
        for f in range(fields):
            value = flat[lines, f * levels : (f + 1) * levels]
            out[r, f] = value
            if edges:
                wide = value.astype(F32)
                begin, end = wide[0:1], wide[width - 1 : width]
                rims[2][r, f : f + 1] = jnp.where(even_lon, end, begin)
                rims[3][r, f : f + 1] = jnp.where(even_lon, begin, end)
        return 0

    lax.fori_loop(0, rows, row, 0)
    if edges:
        even = pos[1] % 2 == 0
        rims[0][...] = out[jnp.where(even, rows - 1, 0)]
        rims[1][...] = out[jnp.where(even, 0, rows - 1)]


def collect(slot, pos, owners, answers, shape, edges):
    places = tuple(place for _, place in answers)
    answers = [answer for answer, _ in answers]
    rows, fields, width, levels = shape
    outs = [jax.ShapeDtypeStruct(shape, BF16)]
    if edges:
        outs += [jax.ShapeDtypeStruct((fields, width, levels), BF16)] * 2
        outs += [jax.ShapeDtypeStruct((rows, fields, levels), F32)] * 2
    return pl.pallas_call(
        functools.partial(collect_kernel, slot, places, edges),
        out_shape=outs,
        in_specs=[SMEM, SMEM] + [VMEM] * len(answers),
        out_specs=[VMEM] * len(outs),
        scratch_shapes=[pltpu.VMEM((rows * width, fields * levels), BF16)],
        compiler_params=params(16),
    )(pos, owners, *answers)


def shards(state, background, diffusivity, radiances, owners, first_layer, second_layer, third_layer, channel_weight):
    n_lon, n_lat = lax.axis_size("lon"), lax.axis_size("lat")
    served = min(SERVED, n_lon)
    group = n_lon // served
    slots, _, blocks = owners.shape
    rows, width, _, _ = state.shape
    span = rows * width // blocks
    h1, h2 = first_layer.shape[2], second_layer.shape[2]
    pos = jnp.stack([lax.axis_index("lon"), lax.axis_index("lat")]).astype(jnp.int32)
    owners = owners[:, 0]
    hits = owners[:, None, :] == jnp.arange(n_lon, dtype=jnp.int32)[None, :, None]
    table = jnp.sum(jnp.where(hits, jnp.arange(blocks, dtype=jnp.int32), 0), axis=2)
    state = state.transpose(0, 2, 1, 3)
    background = background.transpose(0, 2, 1, 3)
    radiances = radiances.reshape(slots, rows * width, -1)
    own = (first_layer[0], second_layer[0], third_layer[0], channel_weight)

    rims = halo_of_state(state, diffusivity)
    gathered = spread_weights(pack_weights(pos, own, n_lat), group, n_lon, n_lat)
    sent = send_radiances(pos, table, radiances, group, served, span)
    got_radiances = [exchange(a, "lon", c) for c, a in enumerate(sent, 1)]
    wide, first, columns, *sent = forward(pos, table, state, diffusivity, rims, group, served, span)
    got_columns = [exchange(a, "lon", c) for c, a in enumerate(sent, 1)]

    answers = {s: [] for s in range(slots)}
    for w in range(served):
        weights = own if w == 0 else [gathered[w][k] for k in range(n_lat)]
        for chosen in [(s,) for s in reversed(range(slots))] if w == served - 1 else [tuple(range(slots))]:
            mine, *theirs = instrument(
                pos, table, columns, radiances, got_columns, got_radiances, weights, group, w, n_lat, (h1, h2), span, chosen
            )
            back = [exchange(a, "lon", c) for c, a in enumerate(theirs, 1)]
            for place, s in enumerate(chosen):
                answers[s] += [(mine, place)] + [(a, place) for a in back]
    shape = state.shape
    late, *edges = collect(1, pos, owners, answers[1], shape, True)
    (early,) = collect(0, pos, owners, answers[0], shape, False)
    costate, edges = backward_first(pos, late, halo_of_adjoint(edges), first, wide, early)
    gradient = backward_last(pos, costate, halo_of_adjoint(edges), wide, state, background)
    return gradient.transpose(0, 2, 1, 3)


def solution(mesh):
    placed = (
        P("lat", "lon", None, None),
        P("lat", "lon", None, None),
        P("lat", "lon", None),
        P(None, "lat", "lon", None),
        P(None, "lat", "lon"),
        P("lon", None, None),
        P("lon", None, None),
        P("lon", None, None),
        P("lon", None),
    )
    return jax.shard_map(shards, mesh=mesh, in_specs=placed, out_specs=P("lat", "lon", None, None), check_vma=False)
```

```python
import functools
import jax
import jax.numpy as jnp
from jax import lax
from jax.experimental import pallas as pl
from jax.experimental.pallas import tpu as pltpu
from jax.sharding import PartitionSpec as P


ADVECTION = 0.25
VERTICAL = 0.1
SERVED = 4
EDGE = 16
SIDE = 8
TAIL = 16
ANY = pl.BlockSpec(memory_space=pl.ANY)
SMEM = pl.BlockSpec(memory_space=pltpu.SMEM)
VMEM = pl.BlockSpec(memory_space=pltpu.VMEM)
F32 = jnp.float32
BF16 = jnp.bfloat16


def params(mib):
    return pltpu.CompilerParams(vmem_limit_bytes=mib << 20)


def exchange(array, axis, mask):
    count = lax.axis_size(axis)
    return lax.ppermute(array, axis, [(i, i ^ mask) for i in range(count)])


def shifted(array, axis, step, periodic):
    count = lax.axis_size(axis)
    pairs = [(i, (i + step) % count) for i in range(count)]
    if not periodic:
        pairs = [(i, j) for i, j in pairs if j == i + step]
    return lax.ppermute(array, axis, pairs)


def paired(array, axis, start, periodic):
    count = lax.axis_size(axis)
    pairs = []
    for i in range(start, count if periodic else count - 1, 2):
        pairs += [(i, (i + 1) % count), ((i + 1) % count, i)]
    return lax.ppermute(array, axis, pairs)


def bits_down(size):
    bit = size // 2
    while bit:
        yield bit
        bit //= 2


def packed_rows(w1, w2, w3, n_lat):
    return (w1.shape[0] // n_lat, w2.shape[0] // n_lat, w3.shape[0] * w3.shape[1] // (w2.shape[1] * n_lat), TAIL)


def fetches(sources, bounds, first, last, lanes, target, base):
    for source, (low, high) in zip(sources, bounds):
        a, b = max(first, low), min(last, high)
        if a < b:
            begin = base + (a - first)
            if not isinstance(begin, int):
                begin = pl.multiple_of(begin, 16)
            yield source.at[pl.ds(a - low, b - a), lanes], target.at[pl.ds(begin, b - a)]


def pack_kernel(n_lat, bounds, pos, w1, w2, w3, scale, *refs):
    *outs, sems = refs
    lat = pos[1]
    width = outs[0].shape[1]
    r1, r2, piece, _ = packed_rows(w1, w2, w3, n_lat)
    parts = width // w3.shape[1]
    ends = (r1, r1 + r2, r1 + r2 + piece, r1 + r2 + piece + TAIL)
    copies = []

    def put(first, last, lanes, source, base):
        for at, onto in fetches(outs, bounds, first, last, lanes, source, base):
            copies.append(pltpu.make_async_copy(onto, at, sems.at[len(copies)]))

    everything = pl.ds(0, width)
    put(0, ends[0], everything, w1, lat * r1)
    put(ends[0], ends[1], everything, w2, lat * r2)
    for j in range(parts):
        put(ends[1], ends[2], pl.ds(j * w3.shape[1], w3.shape[1]), w3, (lat * parts + j) * piece)
    for copy in copies:
        copy.start()
    whole = scale[...]
    high = whole.astype(BF16).astype(F32)
    rest = whole - high
    middle = rest.astype(BF16).astype(F32)
    low = rest - middle
    rows = lax.broadcasted_iota(jnp.int32, (TAIL, scale.shape[1]), 0)
    stacked = jnp.where(rows == 0, high, jnp.where(rows == 1, middle, low))
    for out, (low_row, high_row) in zip(outs, bounds):
        if high_row == ends[3]:
            tail = slice(ends[2] - low_row, ends[3] - low_row)
            out[tail] = jnp.zeros((TAIL, width), BF16)
            out[tail, 0 : scale.shape[1]] = jnp.where(rows < 3, stacked, 0.0).astype(BF16)
    for copy in copies:
        copy.wait()


def pack_weights(pos, weights, n_lat):
    w1, w2, w3, scale = weights
    width = w1.shape[1]
    rows = sum(packed_rows(w1, w2, w3, n_lat))
    half = rows // (2 * TAIL) * TAIL
    bounds = ((0, half), (half, rows))
    return pl.pallas_call(
        functools.partial(pack_kernel, n_lat, bounds),
        out_shape=[jax.ShapeDtypeStruct((b - a, width), BF16) for a, b in bounds],
        in_specs=[SMEM, ANY, ANY, ANY, VMEM],
        out_specs=[VMEM] * len(bounds),
        scratch_shapes=[pltpu.SemaphoreType.DMA((16,))],
        name="pack",
    )(pos, w1, w2, w3, scale)


def spread_weights(packed, group, n_lon, n_lat):
    found = {0: packed}
    bits = sorted(bits_down(n_lon // group))
    for bit in bits:
        found[bit] = tuple(exchange(a, "lon", bit * group) for a in packed)
    for far in range(n_lon // group):
        if far not in found:
            bottom = far & -far
            found[far] = tuple(exchange(a, "lon", bottom * group) for a in found[far ^ bottom])
    gathered = {}
    for served in sorted(found):
        if served == 0:
            continue
        parts = {0: found[served]}
        nearest = served & -served
        for bit in bits_down(n_lat):
            for near in list(parts):
                *early, last = parts[near]
                chunks = [exchange(a, "lat", bit) for a in early]
                if near == 0 and bit == n_lat // 2 and served != nearest:
                    joined = gathered[served ^ nearest][bit][-1]
                    chunks.append(exchange(joined, "lon", nearest * group))
                else:
                    chunks.append(exchange(last, "lat", bit))
                parts[near | bit] = tuple(chunks)
        gathered[served] = parts
    return gathered


def radiance_kernel(group, pos, table, source, *outs):
    slots, served, span, _ = outs[0].shape
    for c, out in enumerate(outs, 1):
        for s in range(slots):
            for w in range(served):
                block = table[s, pos[0] ^ (w * group + c)]
                out[s, w] = source[s, pl.ds(pl.multiple_of(block * span, span), span)]


def send_radiances(pos, table, radiances, group, served, span):
    slots, _, channels = radiances.shape
    shape = jax.ShapeDtypeStruct((slots, served, span, channels), BF16)
    return pl.pallas_call(
        functools.partial(radiance_kernel, group),
        out_shape=[shape] * (group - 1),
        in_specs=[SMEM, SMEM, VMEM],
        out_specs=[VMEM] * (group - 1),
        name="pick_radiances",
    )(pos, table, radiances)


def vertical_sum(values):
    lane = lax.broadcasted_iota(jnp.int32, values.shape, 1)
    size = values.shape[1]
    upper = jnp.where(lane == size - 1, 0.0, pltpu.roll(values, size - 1, 1))
    lower = jnp.where(lane == 0, 0.0, pltpu.roll(values, 1, 1))
    return upper + lower


def step_value(centre, east, west, north, south, zonal, meridional, kappa):
    transport = 0.5 * ADVECTION * (zonal * (east - west) + meridional * (north - south))
    spread = east + west + north + south - 4.0 * centre
    return centre - transport + kappa * spread + VERTICAL * (vertical_sum(centre) - 2.0 * centre)


def forward_kernel(group, pos, table, state, kappa, south, north, west, east, wide, first, columns, *sends):
    rows, fields, width, levels = state.shape
    inner = pl.ds(EDGE, width)

    def place(r, _):
        wide[r + 2, 0:fields, inner] = state[r]
        wide[r + 2, fields, inner] = kappa[r]
        return 0

    lax.fori_loop(0, rows, place, 0)
    for r in range(2):
        for target, source in ((r, south), (rows + 2 + r, north)):
            wide[target, :, inner] = source[r, :, 0:width]
            wide[target, :, EDGE - 2 : EDGE] = source[r, :, width : width + 2]
            wide[target, :, EDGE + width : EDGE + width + 2] = source[r, :, width + 2 : width + 4]

    def rims(r, _):
        wide[r + 2, :, EDGE - 2 : EDGE] = west[r]
        wide[r + 2, :, EDGE + width : EDGE + width + 2] = east[r]
        return 0

    lax.fori_loop(0, rows, rims, 0)
    low = EDGE - SIDE
    span = width + 2 * SIDE

    def first_row(r, _):
        zonal = wide[r + 1, 0, pl.ds(low, span)]
        meridional = wide[r + 1, 1, pl.ds(low, span)]
        k = wide[r + 1, fields, pl.ds(low, span)]
        for f in range(fields):
            first[r, f] = step_value(
                wide[r + 1, f, pl.ds(low, span)],
                wide[r + 1, f, pl.ds(low + 1, span)],
                wide[r + 1, f, pl.ds(low - 1, span)],
                wide[r + 2, f, pl.ds(low, span)],
                wide[r, f, pl.ds(low, span)],
                zonal,
                meridional,
                k,
            )
        return 0

    lax.fori_loop(0, rows + 2, first_row, 0)

    def second_row(r, _):
        here = pl.ds(SIDE, width)
        zonal = first[r + 1, 0, here]
        meridional = first[r + 1, 1, here]
        k = wide[r + 2, fields, inner]
        lines = pl.ds(pl.multiple_of(r * width, width), width)
        for f in range(fields):
            centre = first[r + 1, f, here]
            value = step_value(
                centre,
                first[r + 1, f, pl.ds(SIDE + 1, width)],
                first[r + 1, f, pl.ds(SIDE - 1, width)],
                first[r + 2, f, here],
                first[r, f, here],
                zonal,
                meridional,
                k,
            )
            columns[0, lines, f * levels : (f + 1) * levels] = centre.astype(BF16)
            columns[1, lines, f * levels : (f + 1) * levels] = value.astype(BF16)
        return 0

    lax.fori_loop(0, rows, second_row, 0)
    slots, served, block, _ = sends[0].shape
    for c, send in enumerate(sends, 1):
        for s in range(slots):
            for w in range(served):
                b = table[s, pos[0] ^ (w * group + c)]
                send[s, w] = columns[s, pl.ds(pl.multiple_of(b * block, block), block)]


def forward(pos, table, state, kappa, rims, group, served, block):
    rows, fields, width, levels = state.shape
    slots = table.shape[0]
    outs = [
        jax.ShapeDtypeStruct((rows + 4, fields + 1, width + 2 * EDGE, levels), F32),
        jax.ShapeDtypeStruct((rows + 2, fields, width + 2 * SIDE, levels), F32),
        jax.ShapeDtypeStruct((slots, rows * width, fields * levels), BF16),
    ] + [jax.ShapeDtypeStruct((slots, served, block, fields * levels), BF16)] * (group - 1)
    return pl.pallas_call(
        functools.partial(forward_kernel, group),
        out_shape=outs,
        in_specs=[SMEM, SMEM] + [VMEM] * 6,
        out_specs=[VMEM] * len(outs),
        compiler_params=params(16),
        name="forward",
    )(pos, table, state, kappa, *rims)


def halo_of_state(state, kappa):
    width = state.shape[2]

    def cut(rows, columns):
        return jnp.concatenate([state[rows, :, columns], kappa[rows, None, columns]], axis=1)

    every = slice(None)
    west = shifted(cut(every, slice(width - 2, width)), "lon", 1, True)
    east = shifted(cut(every, slice(0, 2)), "lon", -1, True)

    def edge(rows):
        return jnp.concatenate([cut(rows, every), west[rows], east[rows]], axis=2)

    south = shifted(edge(slice(-2, None)), "lat", 1, False)
    north = shifted(edge(slice(0, 2)), "lat", -1, False)
    return south, north, west, east


def backward_kernel(first_half, *refs):
    if first_half:
        pos, adj, inner_row, outer_row, close, distant, base, kappa, extra, out, lo, hi, we, ea, pad = refs
        shift, row0 = SIDE, 0
    else:
        pos, adj, inner_row, outer_row, close, distant, base, extra, other, result, out, pad, sems = refs
        shift, row0 = EDGE, 1
    rows, fields, width, levels = adj.shape
    inner = pl.ds(EDGE, width)
    even_lon = pos[0] % 2 == 0

    def place(r, _):
        pad[r + 1, :, inner] = adj[r].astype(F32)
        one, two = close[r], distant[r]
        pad[r + 1, :, EDGE - 1 : EDGE] = jnp.where(even_lon, two, one)[:, None]
        pad[r + 1, :, EDGE + width : EDGE + width + 1] = jnp.where(even_lon, one, two)[:, None]
        return 0

    lax.fori_loop(0, rows, place, 0)
    even = pos[1] % 2 == 0
    pad[jnp.where(even, rows + 1, 0), :, inner] = inner_row[...].astype(F32)
    pad[jnp.where(even, 0, rows + 1), :, inner] = outer_row[...].astype(F32)
    half = 0.5 * ADVECTION

    def diffusion(r, at):
        if first_half:
            return kappa[r + 1, 0, pl.ds(EDGE + at, width)]
        return base[r + 1, fields, pl.ds(EDGE + at, width)]

    def wind(r, f, at):
        return base[r + row0, f, pl.ds(shift + at, width)]

    def row(r, _):
        c_here = (1.0 - 2.0 * VERTICAL) - 4.0 * diffusion(r + 1, 0)
        c_west = diffusion(r + 1, -1) - half * wind(r + 1, 0, -1)
        c_east = diffusion(r + 1, 1) + half * wind(r + 1, 0, 1)
        c_south = diffusion(r, 0) - half * wind(r, 1, 0)
        c_north = diffusion(r + 2, 0) + half * wind(r + 2, 1, 0)
        zonal = jnp.zeros((width, levels), F32)
        meridional = jnp.zeros((width, levels), F32)
        for f in range(fields):
            here = pad[r + 1, f, inner]
            zonal += here * (wind(r + 1, f, 1) - wind(r + 1, f, -1))
            meridional += here * (wind(r + 2, f, 0) - wind(r, f, 0))
        for f in range(fields):
            here = pad[r + 1, f, inner]
            value = (
                here * c_here
                + pad[r + 1, f, pl.ds(EDGE - 1, width)] * c_west
                + pad[r + 1, f, pl.ds(EDGE + 1, width)] * c_east
                + pad[r, f, inner] * c_south
                + pad[r + 2, f, inner] * c_north
                + VERTICAL * vertical_sum(here)
            )
            if f == 0:
                value -= half * zonal
            if f == 1:
                value -= half * meridional
            if first_half:
                value += extra[r, f].astype(F32)
                begin, end = value[0:1], value[width - 1 : width]
                we[r, f : f + 1] = jnp.where(even_lon, end, begin)
                ea[r, f : f + 1] = jnp.where(even_lon, begin, end)
            else:
                value += extra[r, f] - other[r, f]
            out[r, f] = value
        if not first_half:
            pltpu.make_async_copy(out.at[r], result.at[r], sems.at[r]).start()
        return 0

    lax.fori_loop(0, rows, row, 0)
    if not first_half:
        for r in range(rows):
            pltpu.make_async_copy(out.at[r], result.at[r], sems.at[r]).wait()
    if first_half:
        lo[...] = out[jnp.where(even, rows - 1, 0)]
        hi[...] = out[jnp.where(even, 0, rows - 1)]


def halo_of_adjoint(edges):
    inner, outer, close, distant = edges
    return (
        paired(inner, "lat", 0, False),
        paired(outer, "lat", 1, False),
        paired(close, "lon", 0, True),
        paired(distant, "lon", 1, True),
    )


def backward_first(pos, adjoint, rims, first, wide, forcing):
    rows, fields, width, levels = adjoint.shape
    line = jax.ShapeDtypeStruct((fields, width, levels), F32)
    side = jax.ShapeDtypeStruct((rows, fields, levels), F32)
    kappa_spec = pl.BlockSpec(
        (rows + 4, 1, width + 2 * EDGE, levels), lambda i: (0, fields, 0, 0)
    )

    def whole(shape):
        return pl.BlockSpec(shape, lambda i: (0,) * len(shape))

    out, *edges = pl.pallas_call(
        functools.partial(backward_kernel, True),
        grid=(1,),
        out_shape=[jax.ShapeDtypeStruct(adjoint.shape, F32), line, line, side, side],
        in_specs=[SMEM]
        + [whole(a.shape) for a in (adjoint, *rims, first)]
        + [kappa_spec, whole(forcing.shape)],
        out_specs=[whole(adjoint.shape), whole(line.shape), whole(line.shape), whole(side.shape), whole(side.shape)],
        scratch_shapes=[pltpu.VMEM((rows + 2, fields, width + 2 * EDGE, levels), F32)],
        compiler_params=params(16),
        name="backward_first",
    )(pos, adjoint, *rims, first, wide, forcing)
    return out, edges


def backward_last(pos, adjoint, rims, wide, state, background):
    rows, fields, width, levels = adjoint.shape
    return pl.pallas_call(
        functools.partial(backward_kernel, False),
        out_shape=jax.ShapeDtypeStruct(adjoint.shape, F32),
        in_specs=[SMEM] + [VMEM] * 8,
        out_specs=ANY,
        scratch_shapes=[
            pltpu.VMEM((rows, fields, width, levels), F32),
            pltpu.VMEM((rows + 2, fields, width + 2 * EDGE, levels), F32),
            pltpu.SemaphoreType.DMA((rows,)),
        ],
        compiler_params=params(16),
        name="backward_last",
    )(pos, adjoint, *rims, wide, state, background)


def nt_dot(a, b):
    return lax.dot_general(a, b, (((1,), (1,)), ((), ())), preferred_element_type=F32)


def instrument_kernel(group, served, n_lat, chosen, bounds, pos, table, columns, radiances, *refs):
    others = group - 1
    got_columns, refs = refs[:others], refs[others:]
    got_radiances, refs = refs[:others], refs[others:]
    own_weights = served == 0
    n_weights = 4 if own_weights else n_lat * len(bounds)
    weights, refs = refs[:n_weights], refs[n_weights:]
    outs, refs = refs[:group], refs[group:]
    x, y, a1, s1, a2, s2, mis, *built = refs
    slots, span, _ = outs[0].shape
    tile = 256
    for c in range(group):
        for k, s in enumerate(chosen):
            j = c * slots + k
            lines = slice(j * span, (j + 1) * span)
            if c == 0:
                block = table[s, pos[0] ^ (served * group)]
                at = pl.ds(pl.multiple_of(block * span, span), span)
                x[lines] = columns[s, at]
                y[lines] = radiances[s, at]
            else:
                x[lines] = got_columns[c - 1][s, served]
                y[lines] = got_radiances[c - 1][s, served]
    if own_weights:
        w1, w2, w3, scale = weights
        factor = scale[...]
    else:
        w1, w2, w3 = built
        r1, r2, piece, _ = packed_rows(w1, w2, w3, n_lat)
        parts = w2.shape[1] // w3.shape[1]
        ends = (r1, r1 + r2, r1 + r2 + piece)
        everything = pl.ds(0, w1.shape[1])

        def fetch(first, last, lanes, target, base):
            for source, onto in fetches(sources, bounds, first, last, lanes, target, base):
                onto[...] = source[...]

        for near in range(n_lat):
            lat = pos[1] ^ near
            sources = weights[near * len(bounds) : (near + 1) * len(bounds)]
            fetch(0, ends[0], everything, w1, lat * r1)
            fetch(ends[0], ends[1], everything, w2, lat * r2)
            for p in range(parts):
                fetch(ends[1], ends[2], pl.ds(p * w3.shape[1], w3.shape[1]), w3, (lat * parts + p) * piece)
        last, low = weights[len(bounds) - 1], bounds[-1][0]
        triple = last[ends[2] - low : ends[2] - low + TAIL, 0 : w3.shape[1]].astype(F32)
        factor = triple[0:1] + triple[1:2] + triple[2:3]

    def hidden(source, weight, act, slope):
        def column(n, _):
            at = pl.ds(pl.multiple_of(n * tile, tile), tile)
            z = jnp.dot(source[...], weight[:, at], preferred_element_type=F32)
            half = 0.5 * jnp.tanh(0.5 * z)
            sigma = 0.5 + half
            value = z * sigma
            act[:, at] = value.astype(BF16)
            slope[:, at] = sigma + value * (0.5 - half)
            return 0

        lax.fori_loop(0, weight.shape[1] // tile, column, 0, unroll=True)

    hidden(x, w1, a1, s1)
    hidden(a1, w2, a2, s2)
    for n in range(w3.shape[1] // tile):
        at = slice(n * tile, (n + 1) * tile)
        evolved = jnp.dot(a2[...], w3[:, at], preferred_element_type=F32)
        mis[:, at] = (factor[:, at] * (evolved - y[:, at].astype(F32))).astype(BF16)

    def back(source, weight, slope, grad):
        def column(n, _):
            at = pl.ds(pl.multiple_of(n * tile, tile), tile)
            grad[:, at] = (nt_dot(source[...], weight[at]) * slope[:, at]).astype(BF16)
            return 0

        lax.fori_loop(0, weight.shape[0] // tile, column, 0, unroll=True)

    back(mis, w3, s2, a2)
    back(a2, w2, s1, a1)
    for n in range(w1.shape[0] // tile):
        at = slice(n * tile, (n + 1) * tile)
        value = nt_dot(a1[...], w1[at]).astype(BF16)
        for j in range(group * slots):
            outs[j // slots][j % slots, :, at] = value[j * span : (j + 1) * span]


def instrument(pos, table, columns, radiances, got_columns, got_radiances, weights, group, served, n_lat, sizes, span, chosen):
    cin, ch = columns.shape[2], radiances.shape[2]
    slots = len(chosen)
    h1, h2 = sizes
    own = served == 0
    bounds = []
    if not own:
        for chunk in weights[0]:
            low = bounds[-1][1] if bounds else 0
            bounds.append((low, low + chunk.shape[0]))
        weights = [chunk for near in range(n_lat) for chunk in weights[near]]
    lines = group * slots * span
    out = jax.ShapeDtypeStruct((slots, span, cin), BF16)
    return pl.pallas_call(
        functools.partial(instrument_kernel, group, served, n_lat, chosen, tuple(bounds)),
        out_shape=[out] * group,
        in_specs=[SMEM, SMEM] + [VMEM] * (2 + 2 * (group - 1) + len(weights)),
        out_specs=[VMEM] * group,
        scratch_shapes=[
            pltpu.VMEM((lines, cin), BF16),
            pltpu.VMEM((lines, ch), BF16),
            pltpu.VMEM((lines, h1), BF16),
            pltpu.VMEM((lines, h1), F32),
            pltpu.VMEM((lines, h2), BF16),
            pltpu.VMEM((lines, h2), F32),
            pltpu.VMEM((lines, ch), BF16),
        ]
        + ([] if own else [pltpu.VMEM(shape, BF16) for shape in ((cin, h1), (h1, h2), (h2, ch))]),
        compiler_params=params(14 + 2 * (group - 1)),
        cost_estimate=pl.CostEstimate(
            flops=4 * lines * (cin * h1 + h1 * h2 + h2 * ch),
            transcendentals=lines * (h1 + h2),
            bytes_accessed=2 * (cin * h1 + h1 * h2 + h2 * ch + lines * (2 * cin + ch)),
        ),
    )(pos, table, columns, radiances, *got_columns, *got_radiances, *weights)


def collect_kernel(slot, places, edges, pos, owners, *refs):
    outs = 5 if edges else 1
    *answers, flat = refs[: len(refs) - 1 - outs] + refs[len(refs) - 1 :]
    out, *rims = refs[len(answers) : len(answers) + outs]
    rows, fields, width, levels = out.shape
    span = answers[0].shape[1]

    def block(b, _):
        apart = owners[slot, b] ^ pos[0]
        for k, answer in enumerate(answers):

            @pl.when(apart == k)
            def _():
                flat[pl.ds(pl.multiple_of(b * span, span), span)] = answer[places[k]]

        return 0

    lax.fori_loop(0, rows * width // span, block, 0)
    even_lon = pos[0] % 2 == 0

    def row(r, _):
        lines = pl.ds(pl.multiple_of(r * width, width), width)
        for f in range(fields):
            value = flat[lines, f * levels : (f + 1) * levels]
            out[r, f] = value
            if edges:
                wide = value.astype(F32)
                begin, end = wide[0:1], wide[width - 1 : width]
                rims[2][r, f : f + 1] = jnp.where(even_lon, end, begin)
                rims[3][r, f : f + 1] = jnp.where(even_lon, begin, end)
        return 0

    lax.fori_loop(0, rows, row, 0)
    if edges:
        even = pos[1] % 2 == 0
        rims[0][...] = out[jnp.where(even, rows - 1, 0)]
        rims[1][...] = out[jnp.where(even, 0, rows - 1)]


def collect(slot, pos, owners, answers, shape, edges):
    places = tuple(place for _, place in answers)
    answers = [answer for answer, _ in answers]
    rows, fields, width, levels = shape
    outs = [jax.ShapeDtypeStruct(shape, BF16)]
    if edges:
        outs += [jax.ShapeDtypeStruct((fields, width, levels), BF16)] * 2
        outs += [jax.ShapeDtypeStruct((rows, fields, levels), F32)] * 2
    return pl.pallas_call(
        functools.partial(collect_kernel, slot, places, edges),
        out_shape=outs,
        in_specs=[SMEM, SMEM] + [VMEM] * len(answers),
        out_specs=[VMEM] * len(outs),
        scratch_shapes=[pltpu.VMEM((rows * width, fields * levels), BF16)],
        compiler_params=params(16),
    )(pos, owners, *answers)


def shards(state, background, diffusivity, radiances, owners, first_layer, second_layer, third_layer, channel_weight):
    n_lon, n_lat = lax.axis_size("lon"), lax.axis_size("lat")
    served = min(SERVED, n_lon)
    group = n_lon // served
    slots, _, blocks = owners.shape
    rows, width, _, _ = state.shape
    span = rows * width // blocks
    h1, h2 = first_layer.shape[2], second_layer.shape[2]
    pos = jnp.stack([lax.axis_index("lon"), lax.axis_index("lat")]).astype(jnp.int32)
    owners = owners[:, 0]
    hits = owners[:, None, :] == jnp.arange(n_lon, dtype=jnp.int32)[None, :, None]
    table = jnp.sum(jnp.where(hits, jnp.arange(blocks, dtype=jnp.int32), 0), axis=2)
    state = state.transpose(0, 2, 1, 3)
    background = background.transpose(0, 2, 1, 3)
    radiances = radiances.reshape(slots, rows * width, -1)
    own = (first_layer[0], second_layer[0], third_layer[0], channel_weight)

    rims = halo_of_state(state, diffusivity)
    gathered = spread_weights(pack_weights(pos, own, n_lat), group, n_lon, n_lat)
    sent = send_radiances(pos, table, radiances, group, served, span)
    got_radiances = [exchange(a, "lon", c) for c, a in enumerate(sent, 1)]
    wide, first, columns, *sent = forward(pos, table, state, diffusivity, rims, group, served, span)
    got_columns = [exchange(a, "lon", c) for c, a in enumerate(sent, 1)]

    answers = {s: [] for s in range(slots)}
    for w in range(served):
        weights = own if w == 0 else [gathered[w][k] for k in range(n_lat)]
        for chosen in [(s,) for s in reversed(range(slots))] if w == served - 1 else [tuple(range(slots))]:
            mine, *theirs = instrument(
                pos, table, columns, radiances, got_columns, got_radiances, weights, group, w, n_lat, (h1, h2), span, chosen
            )
            back = [exchange(a, "lon", c) for c, a in enumerate(theirs, 1)]
            for place, s in enumerate(chosen):
                answers[s] += [(mine, place)] + [(a, place) for a in back]
    shape = state.shape
    late, *edges = collect(1, pos, owners, answers[1], shape, True)
    (early,) = collect(0, pos, owners, answers[0], shape, False)
    costate, edges = backward_first(pos, late, halo_of_adjoint(edges), first, wide, early)
    gradient = backward_last(pos, costate, halo_of_adjoint(edges), wide, state, background)
    return gradient.transpose(0, 2, 1, 3)


def solution(mesh):
    placed = (
        P("lat", "lon", None, None),
        P("lat", "lon", None, None),
        P("lat", "lon", None),
        P(None, "lat", "lon", None),
        P(None, "lat", "lon"),
        P("lon", None, None),
        P("lon", None, None),
        P("lon", None, None),
        P("lon", None),
    )
    return jax.shard_map(shards, mesh=mesh, in_specs=placed, out_specs=P("lat", "lon", None, None), check_vma=False)
```
